32 devices in a mesh: dp: 2 (over core), context: 4 (over y, x), tensor: 4 (over z).
Axes of the slice: x: 2, y: 2, z: 4, core: 2. Of those that a mesh axis runs over, the one named last changes fastest.
Arguments:
- ids: int32 [4096], P(('dp', 'context', 'tensor')), parts along dimension 0, may hold values from 65 to 84, as said below
- block_order: int32 [16], P('dp'), parts along dimension 0, may hold values from 0 to 7, each once
- embed: bfloat16 [512, 4096], replicated, may hold values from -6 to 6
- mix_gain: float32 [4096], replicated, may hold values from 0.5 to 2
- in_proj: bfloat16 [3, 4096, 2048], P(None, None, 'tensor'), may hold values from -0.09375 to 0.09375
- short_filter: float32 [3, 3, 2048], P(None, None, 'tensor'), may hold values from -1 to 1
- long_filter: float32 [128, 128], P('tensor'), as said below
- conv_skip: float32 [2048], P('tensor'), may hold values from -1 to 1
- hyena_out: bfloat16 [2048, 4096], P('tensor'), may hold values from -0.125 to 0.125
- attn_gain: float32 [4096], replicated, may hold values from 0.5 to 2
- qkv_proj: bfloat16 [3, 4096, 2048], P(None, None, 'tensor'), as said below
- attn_out: bfloat16 [2048, 4096], P('tensor'), may hold values from -0.5 to 0.5
Outputs:
- stream_out: float32 [4096, 4096], P(('dp', 'context', 'tensor')), parts along dimension 0
The draws below stay inside these ranges and needn't reach their ends.
There are 2 independent parts, one for each index of `dp`. The reference program is written for one: setup_inputs(seed, part) draws one part's arguments, and reference() takes and returns one part's arrays. A program takes and returns all parts, laid end to end along the dimension named above; an argument that names none is the same for every part. Nothing has to cross between parts.
Inputs may be any that keep to these rules, and one draw needn't show every extreme that they name: `ids`: every id is the code of a base: 65, 67, 71 or 84. `block_order`: every block lies in exactly one slot. `long_filter`: real-valued filter taps. `qkv_proj`: real-valued projection weights.
All inputs are finite; a program needn't handle non-finite values.
Results may differ from the reference program's by a relative error of at most 0.01.
Values may be sent and summed in bfloat16 or wider, within the bound.
No kernel may reach another device: no remote copies, remote signals or barrier semaphores. Data moves between devices by JAX's collectives and lax.ppermute only.
A program may use at most 192 MiB of HBM per device.

```python
import math
import jax
import jax.numpy as jnp
from jax import lax

D = 4096
VOCAB = 512
HEADS = 16
HD = 128
CH = 2048
GROUP_CH = 16
FILT = 128
SHORT = 3
BLK = 256
BLOCKS = 8
SEQ = 2048
GROUPS = 128


def draw_ids(key, part):
    codes = jnp.array([65, 67, 71, 84], dtype=jnp.int32)
    picks = jax.random.randint(key, (SEQ,), 0, 4)
    slots = jnp.arange(SEQ, dtype=jnp.int32)
    picks = jnp.where(slots < 2, slots * 3, picks)
    return jnp.take(codes, picks)


def draw_long_filter(key, part):
    rate_key, tap_key = jax.random.split(key, 2)
    low_rate, high_rate = (0.001, 0.05)
    rates = jnp.exp(jax.random.uniform(rate_key, (GROUPS, 1), jnp.float32, math.log(low_rate), math.log(high_rate)))
    taps = jnp.arange(FILT, dtype=jnp.float32)[None, :]
    scaling = jnp.sqrt((1.0 - jnp.exp(-2.0 * rates)) / (1.0 - jnp.exp(-2.0 * rates * FILT)))
    rough = jnp.clip(jax.random.normal(tap_key, (GROUPS, FILT), jnp.float32), -4.0, 4.0)
    return rough * jnp.exp(-rates * taps) * scaling


def draw_qkv_proj(key, part):
    base = jnp.clip(jax.random.normal(key, (3, D, HEADS * HD), jnp.float32), -5.0, 5.0) / math.sqrt(D)
    queries = 1.6 * base[0]
    keys = base[1]
    return jnp.stack([queries, keys, base[2]]).astype(jnp.bfloat16)


def block_levels(key, dims, cuts, low, largest):
    def one(dim, parts):
        steps = jax.random.uniform(jax.random.fold_in(jax.random.fold_in(key, 6), dim), (parts,), jnp.float32, low / len(cuts), largest / len(cuts))
        return jnp.repeat(jnp.exp(steps), dims[dim] // parts).reshape((-1,) + (1,) * (len(dims) - dim - 1))

    loudness = one(*cuts[0])
    for cut in cuts[1:]:
        loudness = loudness * one(*cut)
    return loudness


def noise(stream_key, shape, deviation, bound, shards=(), held_as=jnp.bfloat16):
    values = jax.random.normal(stream_key, shape, jnp.float32) * deviation
    if len(shards) > 0:
        values = block_levels(stream_key, shape, shards, -0.22, 0.18) * values
    return jnp.clip(values, min=-bound, max=bound).astype(held_as)


def setup_inputs(seed: int = 0, part: int = 0) -> dict:
    key_list = jax.random.split(jax.random.key(seed), 13)
    part_splits = jax.random.split(jax.random.fold_in(key_list[12], part), 13)
    return {
        "ids": draw_ids(jax.random.fold_in(jax.random.fold_in(key_list[12], part), 71), part),
        "block_order": jax.random.permutation(part_splits[1], BLOCKS).astype(jnp.int32),
        "embed": noise(key_list[2], (VOCAB, D), 1.0, 6.0),
        "mix_gain": jnp.clip(jnp.exp(jax.random.uniform(key_list[3], (D,), jnp.float32, math.log(0.5), math.log(2.0))), 0.5, 2.0),
        "in_proj": noise(key_list[4], (3, D, CH), D ** -0.5, 0.09375, ((2, 4),)),
        "short_filter": jnp.clip(jax.random.uniform(key_list[5], (3, SHORT, CH), jnp.float32, -1.0, 1.0) * block_levels(key_list[5], (3, SHORT, CH), ((2, 4),), -0.4, 0.0), -1.0, 1.0),
        "long_filter": draw_long_filter(jax.random.fold_in(key_list[12], 71), part),
        "conv_skip": jnp.clip(jax.random.uniform(key_list[7], (CH,), jnp.float32, -1.0, 1.0) * block_levels(key_list[7], (CH,), ((0, 4),), -0.4, 0.0), -1.0, 1.0),
        "hyena_out": noise(key_list[8], (CH, D), CH ** -0.5, 0.125, ((0, 4),)),
        "attn_gain": jnp.clip(jnp.exp(jax.random.uniform(key_list[9], (D,), jnp.float32, math.log(0.5), math.log(2.0))), 0.5, 2.0),
        "qkv_proj": draw_qkv_proj(jax.random.fold_in(key_list[12], 71), part),
        "attn_out": noise(key_list[11], (HEADS * HD, D), HD ** -0.5, 0.5, ((0, 4),)),
    }


EPS = 1e-06
THETA = 1000000.0
NEG_FILL = -1e+30

def rms_scale(row_data, gain_vec):
    values = row_data.astype(jnp.float32)
    factor = lax.rsqrt(lax.optimization_barrier(jnp.mean(values * values, axis=-1, keepdims=True)) + EPS)
    return (values * factor * gain_vec).astype(jnp.bfloat16)

def toeplitz(long_filter):
    filter_len = long_filter.shape[1]
    tap_lag = jnp.arange(filter_len, dtype=jnp.int32)[:, None] - jnp.arange(filter_len, dtype=jnp.int32)[None, :]
    near_taps = jnp.take(long_filter, jnp.clip(tap_lag, 0, filter_len - 1), axis=1)
    far_taps = jnp.take(long_filter, jnp.clip(tap_lag + filter_len, 0, filter_len - 1), axis=1)
    near_taps = jnp.where(tap_lag[None] >= 0, near_taps, jnp.zeros_like(near_taps))
    far_taps = jnp.where(tap_lag[None] < 0, far_taps, jnp.zeros_like(far_taps))
    return (near_taps, far_taps)

def long_conv(padded, long_filter, group_width):
    filter_len = long_filter.shape[1]
    near_taps, far_taps = toeplitz(long_filter)
    row_total = padded.shape[0]
    chan_total = padded.shape[1]
    blocks = padded.reshape(row_total // filter_len, filter_len, chan_total // group_width, group_width)
    current_part = jnp.einsum('grs,bsgc->brgc', near_taps, blocks[1:], precision=lax.Precision.HIGHEST)
    before = jnp.einsum('grs,bsgc->brgc', far_taps, blocks[:-1], precision=lax.Precision.HIGHEST)
    return (current_part + before).reshape(row_total - filter_len, chan_total)

def short_conv(padded_rows, short_filter, out_len):
    taps = short_filter.shape[1]
    result = jnp.zeros((padded_rows.shape[0], out_len, padded_rows.shape[2]), jnp.float32)
    for tap_at in range(taps):
        offset = taps - 1 - tap_at
        result = result + short_filter[:, tap_at][:, None, :] * padded_rows[:, offset:offset + out_len]
    return result

def rotate(values, positions, head_dim):
    half_dim = head_dim // 2
    inverse_freq = THETA ** (-(2.0 * jnp.arange(half_dim, dtype=jnp.float32)) / head_dim)
    angles = positions.astype(jnp.float32)[:, None] * inverse_freq[None, :]
    cosine_part = jnp.cos(angles)[:, None, :]
    sine_part = jnp.sin(angles)[:, None, :]
    lower_half = values[..., :half_dim]
    upper_half = values[..., half_dim:]
    return jnp.concatenate([lower_half * cosine_part - upper_half * sine_part, upper_half * cosine_part + lower_half * sine_part], axis=-1)

def reference(ids, block_order, embed, mix_gain, in_proj, short_filter, long_filter, conv_skip, hyena_out, attn_gain, qkv_proj, attn_out):
    row_index = jnp.arange(SEQ, dtype=jnp.int32)
    positions = (block_order[row_index // BLK] * BLK + row_index % BLK).astype(jnp.int32)
    ids_true = jnp.zeros((SEQ,), jnp.int32).at[positions].set(ids)
    embedded = embed[ids_true]
    mixed_in = rms_scale(embedded, mix_gain)
    projected = jnp.stack([jnp.dot(mixed_in, in_proj[part_at], preferred_element_type=jnp.float32) for part_at in range(3)]).astype(jnp.bfloat16)
    padded_rows = jnp.concatenate([jnp.zeros((3, SHORT - 1, CH), jnp.float32), projected.astype(jnp.float32)], axis=1)
    filtered = short_conv(padded_rows, short_filter, SEQ)
    gated = filtered[1] * filtered[2]
    padded = jnp.concatenate([jnp.zeros((FILT, CH), jnp.float32), gated], axis=0)
    long_mix = long_conv(padded, long_filter, GROUP_CH)
    hyena_mix = (filtered[0] * (long_mix + conv_skip * gated)).astype(jnp.bfloat16)
    hyena_branch = jnp.dot(hyena_mix, hyena_out, preferred_element_type=jnp.float32)
    stream_mid = embedded.astype(jnp.float32) + hyena_branch
    attn_in = rms_scale(stream_mid, attn_gain)
    projections = [jnp.dot(attn_in, qkv_proj[part_at], preferred_element_type=jnp.float32).reshape(SEQ, HEADS, HD) for part_at in range(3)]
    queries = rotate(projections[0], row_index, HD).astype(jnp.bfloat16)
    keys = rotate(projections[1], row_index, HD).astype(jnp.bfloat16)
    values = projections[2].astype(jnp.bfloat16)

    def head_attend(operands):
        head_q, head_k, head_v = operands
        keys_wide = head_k.astype(jnp.float32)

        def block_attend(row_start):
            query_rows = lax.dynamic_slice_in_dim(head_q, row_start, BLK, 0).astype(jnp.float32)
            scores = jnp.dot(query_rows, keys_wide.T, preferred_element_type=jnp.float32) * HD ** (-0.5)
            query_pos = row_start + jnp.arange(BLK, dtype=jnp.int32)
            visible = jnp.arange(SEQ, dtype=jnp.int32)[None, :] <= query_pos[:, None]
            scores = jnp.where(visible, scores, NEG_FILL)
            top_score = lax.optimization_barrier(jnp.max(scores, axis=-1, keepdims=True))
            weights = jnp.where(visible, jnp.exp(scores - top_score), 0.0)
            totals = lax.optimization_barrier(jnp.sum(weights, axis=-1, keepdims=True))
            mixed = jnp.dot(weights.astype(jnp.bfloat16), head_v, preferred_element_type=jnp.float32)
            return (mixed / totals).astype(jnp.bfloat16)
        starts = jnp.arange(SEQ // BLK, dtype=jnp.int32) * BLK
        return lax.map(block_attend, starts).reshape(SEQ, HD)
    attended = lax.map(head_attend, (queries.transpose(1, 0, 2), keys.transpose(1, 0, 2), values.transpose(1, 0, 2)))
    attended = attended.transpose(1, 0, 2).reshape(SEQ, HEADS * HD)
    attn_branch = jnp.dot(attended, attn_out, preferred_element_type=jnp.float32)
    stream_true = stream_mid + attn_branch
    return stream_true[positions]
```

```python
import math

import jax
import jax.numpy as jnp
from jax import lax
from jax.experimental import pallas as pl
from jax.experimental.pallas import tpu as pltpu
from jax.sharding import PartitionSpec as P

HD = 128
GROUP_CH = 16


EPS = 1e-06
THETA = 1000000.0
NEG_FILL = -1e30


def rms_scale(row_data, gain_vec):
    values = row_data.astype(jnp.float32)
    factor = lax.rsqrt(jnp.mean(values * values, axis=-1, keepdims=True) + EPS)
    return (values * factor * gain_vec).astype(jnp.bfloat16)


def toeplitz(long_filter):
    filter_len = long_filter.shape[1]
    tap_lag = (
        jnp.arange(filter_len, dtype=jnp.int32)[:, None]
        - jnp.arange(filter_len, dtype=jnp.int32)[None, :]
    )
    near_taps = jnp.take(long_filter, jnp.clip(tap_lag, 0, filter_len - 1), axis=1)
    far_taps = jnp.take(long_filter, jnp.clip(tap_lag + filter_len, 0, filter_len - 1), axis=1)
    near_taps = jnp.where(tap_lag[None] >= 0, near_taps, jnp.zeros_like(near_taps))
    far_taps = jnp.where(tap_lag[None] < 0, far_taps, jnp.zeros_like(far_taps))
    return (near_taps, far_taps)


def long_conv(padded, long_filter, group_width):
    filter_len = long_filter.shape[1]
    near_taps, far_taps = toeplitz(long_filter)
    row_total = padded.shape[0]
    chan_total = padded.shape[1]
    blocks = padded.reshape(
        row_total // filter_len, filter_len, chan_total // group_width, group_width
    )
    current_part = jnp.einsum(
        "grs,bsgc->brgc", near_taps, blocks[1:], precision=lax.Precision.HIGHEST
    )
    before = jnp.einsum("grs,bsgc->brgc", far_taps, blocks[:-1], precision=lax.Precision.HIGHEST)
    return (current_part + before).reshape(row_total - filter_len, chan_total)


def short_conv(padded_rows, short_filter, out_len):
    taps = short_filter.shape[1]
    result = jnp.zeros((padded_rows.shape[0], out_len, padded_rows.shape[2]), jnp.float32)
    for tap_at in range(taps):
        offset = taps - 1 - tap_at
        result = (
            result + short_filter[:, tap_at][:, None, :] * padded_rows[:, offset : offset + out_len]
        )
    return result


def rotate(values, positions, head_dim):
    half_dim = head_dim // 2
    inverse_freq = THETA ** (-(2.0 * jnp.arange(half_dim, dtype=jnp.float32)) / head_dim)
    angles = positions.astype(jnp.float32)[:, None] * inverse_freq[None, :]
    cosine_part = jnp.cos(angles)[:, None, :]
    sine_part = jnp.sin(angles)[:, None, :]
    lower_half = values[..., :half_dim]
    upper_half = values[..., half_dim:]
    return jnp.concatenate(
        [
            lower_half * cosine_part - upper_half * sine_part,
            upper_half * cosine_part + lower_half * sine_part,
        ],
        axis=-1,
    )


def generic_body(
    ids,
    block_order,
    embed,
    mix_gain,
    in_proj,
    short_filter,
    long_filter,
    conv_skip,
    hyena_out,
    attn_gain,
    qkv_proj,
    attn_out,
):
    tok_rows = ids.shape[0]
    tensor_count = lax.axis_size("tensor")
    context_count = lax.axis_size("context")
    ctx_rows = tok_rows * tensor_count
    block_rows = ctx_rows // 2
    filter_len = long_filter.shape[1]
    short_len = short_filter.shape[1]
    halo_len = filter_len + short_len - 2
    chan_local = in_proj.shape[2]
    context_at = lax.axis_index("context")
    vocab_ids = jnp.arange(embed.shape[0], dtype=jnp.int32)
    chosen = (ids[:, None] == vocab_ids[None, :]).astype(jnp.bfloat16)
    embedded = jnp.dot(chosen, embed, preferred_element_type=jnp.float32).astype(jnp.bfloat16)
    embedded_all = lax.all_gather(embedded, "tensor", axis=0, tiled=True)
    mixed_in = rms_scale(embedded_all, mix_gain)
    projected = jnp.einsum(
        "rd,jdc->jrc", mixed_in, in_proj, preferred_element_type=jnp.float32
    ).astype(jnp.bfloat16)
    slot_ids = jnp.arange(2 * context_count, dtype=jnp.int32)
    slot_pair = 2 * context_at + jnp.arange(2, dtype=jnp.int32)
    owned_blocks = jnp.sum(
        jnp.where(slot_ids[None, :] == slot_pair[:, None], block_order[None, :], 0), axis=1
    )
    local_pos = (
        owned_blocks[:, None] * block_rows + jnp.arange(block_rows, dtype=jnp.int32)[None, :]
    ).reshape(ctx_rows)
    tail_rows = jnp.stack(
        [projected[:, block_rows - halo_len : block_rows], projected[:, ctx_rows - halo_len :]]
    )
    all_tails = lax.all_gather(tail_rows, "context", axis=0, tiled=True)
    out_len = filter_len - 1 + block_rows
    pieces = []
    for block_at in range(2):
        holder_hit = (block_order == owned_blocks[block_at] - 1).astype(jnp.bfloat16)
        before_rows = jnp.einsum(
            "s,sjrc->jrc", holder_hit, all_tails, preferred_element_type=jnp.float32
        )
        own_rows = projected[:, block_at * block_rows : (block_at + 1) * block_rows].astype(
            jnp.float32
        )
        extended = jnp.concatenate([before_rows, own_rows], axis=1)
        filtered = short_conv(extended, short_filter, out_len)
        gated_rows = filtered[1] * filtered[2]
        padded = jnp.concatenate([jnp.zeros((1, chan_local), jnp.float32), gated_rows], axis=0)
        long_mix = long_conv(padded, long_filter, GROUP_CH)
        own_gate = gated_rows[filter_len - 1 :]
        pieces.append(
            (filtered[0, filter_len - 1 :] * (long_mix + conv_skip * own_gate)).astype(jnp.bfloat16)
        )
    hyena_mix = jnp.concatenate(pieces, axis=0)
    hyena_own = lax.psum_scatter(
        jnp.dot(hyena_mix, hyena_out, preferred_element_type=jnp.float32),
        "tensor",
        scatter_dimension=0,
        tiled=True,
    )
    stream_own = embedded.astype(jnp.float32) + hyena_own
    stream_all = lax.all_gather(stream_own, "tensor", axis=0, tiled=True)
    attn_in = rms_scale(stream_all, attn_gain)
    projections = jnp.einsum("rd,jdf->jrf", attn_in, qkv_proj, preferred_element_type=jnp.float32)
    local_heads = projections.shape[2] // HD
    shaped = projections.reshape(3, ctx_rows, local_heads, HD)
    queries = rotate(shaped[0], local_pos, HD).astype(jnp.bfloat16)
    keys_flat = (
        rotate(shaped[1], local_pos, HD).astype(jnp.bfloat16).reshape(ctx_rows, local_heads * HD)
    )
    values_flat = shaped[2].astype(jnp.bfloat16).reshape(ctx_rows, local_heads * HD)
    score_scale = HD ** (-0.5)
    start_state = (
        jnp.full((2, block_rows, local_heads), NEG_FILL, jnp.float32),
        jnp.zeros((2, block_rows, local_heads), jnp.float32),
        jnp.zeros((2, block_rows, local_heads, HD), jnp.float32),
    )
    key_piece = lax.all_gather(keys_flat, "context", axis=0, tiled=True)
    value_piece = lax.all_gather(values_flat, "context", axis=0, tiled=True)
    piece_len = key_piece.shape[0]
    sub_len = math.gcd(piece_len, 512)

    def attend_sub(sub_index, carried):
        key_block = lax.dynamic_slice_in_dim(key_piece, sub_index * sub_len, sub_len, 0).reshape(
            sub_len, local_heads, HD
        )
        value_block = lax.dynamic_slice_in_dim(
            value_piece, sub_index * sub_len, sub_len, 0
        ).reshape(sub_len, local_heads, HD)
        row_ids = sub_index * sub_len + jnp.arange(sub_len, dtype=jnp.int32)
        holder = row_ids // block_rows
        key_pos = (
            jnp.sum(
                jnp.where(holder[:, None] == slot_ids[None, :], block_order[None, :], 0), axis=1
            )
            * block_rows
            + row_ids % block_rows
        )
        top_all, sums_all, weighted_all = carried
        outputs = []
        for block_at in range(2):
            query_rows = queries[block_at * block_rows : (block_at + 1) * block_rows]
            query_pos = local_pos[block_at * block_rows : (block_at + 1) * block_rows]
            top_score = top_all[block_at]
            weight_sum = sums_all[block_at]
            weighted = weighted_all[block_at]
            scores = (
                jnp.einsum(
                    "qhd,khd->qhk", query_rows, key_block, preferred_element_type=jnp.float32
                )
                * score_scale
            )
            visible = key_pos[None, None, :] <= query_pos[:, None, None]
            scores = jnp.where(visible, scores, NEG_FILL)
            new_top = jnp.maximum(top_score, jnp.max(scores, axis=-1))
            rescale = jnp.exp(top_score - new_top)
            weights = jnp.where(visible, jnp.exp(scores - new_top[..., None]), 0.0)
            weight_sum = weight_sum * rescale + jnp.sum(weights, axis=-1)
            weighted = weighted * rescale[..., None] + jnp.einsum(
                "qhk,khd->qhd",
                weights.astype(jnp.bfloat16),
                value_block,
                preferred_element_type=jnp.float32,
            )
            result = (new_top, weight_sum, weighted)
            outputs.append(result)
        return tuple((jnp.stack([entry[field] for entry in outputs]) for field in range(3)))

    top_final, sums_final, weighted_final = lax.fori_loop(
        0, piece_len // sub_len, attend_sub, start_state
    )
    attended = (
        (weighted_final / sums_final[..., None])
        .astype(jnp.bfloat16)
        .reshape(ctx_rows, local_heads * HD)
    )
    attn_own = lax.psum_scatter(
        jnp.dot(attended, attn_out, preferred_element_type=jnp.float32).astype(jnp.bfloat16),
        "tensor",
        scatter_dimension=0,
        tiled=True,
    ).astype(jnp.float32)
    return stream_own + attn_own


CODES = (65, 67, 71, 84)
BF16 = jnp.bfloat16
F32 = jnp.float32


def swap_axis(value, axis, mask):
    size = lax.axis_size(axis)
    return lax.ppermute(value, axis, [(at, at ^ mask) for at in range(size)])


def rows_of(weights, lane_start, width):
    return lax.dynamic_slice(weights, (0, lane_start), (weights.shape[0], width))


def along_chain(piece, edge_plane):
    middle = [(1, 2), (2, 1)]
    outward = [(1, 0), (2, 3)]
    near = swap_axis(piece, "tensor", 1)
    across = lax.ppermute(piece, "tensor", middle)
    far_mid = lax.ppermute(near, "tensor", middle)
    across_out = lax.ppermute(across, "tensor", outward)
    far_out = lax.ppermute(far_mid, "tensor", outward)
    return (
        near,
        jnp.where(edge_plane, across_out, across),
        jnp.where(edge_plane, far_out, far_mid),
    )


def dot32(left, right):
    return jnp.dot(left, right, preferred_element_type=F32)


def hyena_kernel(coef_ref, hot_ref, taps_ref, skip_ref, mix_ref):
    hot = hot_ref[...]
    first, second, third = (dot32(coef_ref[j], hot) for j in range(3))
    gated = second * third
    packed = gated.astype(BF16)
    row = lax.broadcasted_iota(jnp.int32, (128, 128), 0)
    lane = lax.broadcasted_iota(jnp.int32, (128, 128), 1)
    near = lane >= row
    mixed = []
    for group in range(16):
        spread = jnp.broadcast_to(taps_ref[group : group + 1, :], (128, 128))
        rolled = pltpu.roll(spread, 0, 1, stride=1, stride_axis=0)
        zero = jnp.zeros_like(rolled)
        matrix = jnp.concatenate(
            [jnp.where(near, zero, rolled), jnp.where(near, rolled, zero)], axis=0
        ).astype(BF16)
        chans = packed[16 * group : 16 * group + 16]
        left = jnp.concatenate(
            [chans[:, at : at + 256] for at in (0, 128, 384, 512)], axis=0
        )
        result = dot32(left, matrix)
        mixed.append(jnp.concatenate([result[16 * i : 16 * i + 16] for i in range(4)], axis=1))
    long_mix = jnp.concatenate(mixed, axis=0)
    own_gate = jnp.concatenate([gated[:, 128:384], gated[:, 512:768]], axis=1)
    own_first = jnp.concatenate([first[:, 128:384], first[:, 512:768]], axis=1)
    mix = own_first * (long_mix + skip_ref[...] * own_gate)
    mix_ref[...] = mix.T.astype(BF16)


def hyena_mixes(coef, hot, taps, skip):
    chans = coef.shape[1]
    step = 256
    return pl.pallas_call(
        hyena_kernel,
        grid=(chans // step,),
        in_specs=[
            pl.BlockSpec((3, step, coef.shape[2]), lambda i: (0, i, 0)),
            pl.BlockSpec(hot.shape, lambda i: (0, 0)),
            pl.BlockSpec((step // 16, 128), lambda i: (i, 0)),
            pl.BlockSpec((step, 1), lambda i: (i, 0)),
        ],
        out_specs=pl.BlockSpec((512, step), lambda i: (0, i)),
        out_shape=jax.ShapeDtypeStruct((512, chans), BF16),
        name="hyena_mix",
    )(coef, hot, taps, skip)


VM = pl.BlockSpec(memory_space=pltpu.VMEM)
SM = pl.BlockSpec(memory_space=pltpu.SMEM)


def branch_kernel(where_ref, own_mix_ref, oth_mix_ref, home_ref, *refs):
    parts, (own_ref, oth_ref) = refs[:15], refs[15:]
    for mix_ref, out_ref in ((own_mix_ref, own_ref), (oth_mix_ref, oth_ref)):

        def lefts(unit, start, size):
            base = pl.multiple_of(where_ref[unit] * 512, 512)
            return mix_ref[:, pl.ds(base + start, size)]

        for rel in range(4):
            lane = pl.multiple_of(where_ref[4 + rel] * 512, 512)
            total = dot32(lefts(0, 0, 512), home_ref[:, pl.ds(lane, 512)])
            for unit in range(3):
                block = parts[5 * unit : 5 * unit + 5]
                if rel < 3:
                    total += dot32(lefts(unit + 1, 0, 512), block[rel][...])
                else:
                    total += dot32(lefts(unit + 1, 0, 256), block[3][...])
                    total += dot32(lefts(unit + 1, 256, 256), block[4][...])
            out_ref[:, pl.ds(lane, 512)] = total.astype(out_ref.dtype)


def hyena_branches(where, own_mix, oth_mix, home, parts):
    return pl.pallas_call(
        branch_kernel,
        in_specs=[SM] + [VM] * (3 + len(parts)),
        out_specs=[VM, VM],
        out_shape=[
            jax.ShapeDtypeStruct((512, 2048), F32),
            jax.ShapeDtypeStruct((512, 2048), BF16),
        ],
        name="hyena_branch",
    )(where, own_mix, oth_mix, home, *parts)


def qkv_kernel(
    where_ref, own_ref, oth_ref, hot_ref, base_ref, gain_ref, proj_ref, cos_ref, sin_ref,
    out_ref, rows_ref, total_ref, power_ref, block_ref,
):
    at = pl.program_id(0)

    @pl.when(at == 0)
    def _():
        total_ref[...] = jnp.zeros_like(total_ref)
        power_ref[...] = jnp.zeros_like(power_ref)

    embedded = dot32(hot_ref[...], base_ref[...])

    @pl.when(at < 4)
    def _():
        block_ref[...] = embedded + own_ref[...]

    @pl.when(at >= 4)
    def _():
        block_ref[...] = embedded + oth_ref[...].astype(F32)

    stream = block_ref[...]
    rows_ref[...] = block_ref[pl.ds(pl.multiple_of(where_ref[8] * 128, 128), 128), :]
    power_ref[...] += jnp.sum(stream * stream, axis=1, keepdims=True)
    scaled = (stream * gain_ref[...]).astype(BF16)
    for j in range(3):
        total_ref[:, 512 * j : 512 * j + 512] += dot32(scaled, proj_ref[j])

    @pl.when(at == 7)
    def _():
        factor = lax.rsqrt(power_ref[...] * (1.0 / 4096.0) + EPS)
        cosine = cos_ref[...] * factor
        sine = sin_ref[...] * factor
        for rel in range(4):
            for j in range(3):
                lane = pl.multiple_of(where_ref[9 + rel] * 128 + 512 * j, 128)
                piece = total_ref[:, pl.ds(lane, 128)]
                if j < 2:
                    piece = piece * cosine + pltpu.roll(piece, 64, 1) * sine
                else:
                    piece = piece * factor
                out_ref[rel, :, 128 * j : 128 * j + 128] = piece.astype(BF16)


def qkv_heads(where, own, oth, hot, base, gain, proj, cosine, sine):
    grid_spec = pltpu.PrefetchScalarGridSpec(
        num_scalar_prefetch=1,
        grid=(8,),
        in_specs=[
            pl.BlockSpec((512, 512), lambda i, w: (0, jnp.minimum(i, 3))),
            pl.BlockSpec((512, 512), lambda i, w: (0, jnp.maximum(i - 4, 0))),
            pl.BlockSpec(hot.shape, lambda i, w: (0, 0)),
            pl.BlockSpec((base.shape[0], 512), lambda i, w: (0, w[i])),
            pl.BlockSpec((1, 512), lambda i, w: (0, w[i])),
            pl.BlockSpec((3, 512, 512), lambda i, w: (0, w[i], 0)),
            pl.BlockSpec((512, 128), lambda i, w: (0, 0)),
            pl.BlockSpec((512, 128), lambda i, w: (0, 0)),
        ],
        out_specs=[
            pl.BlockSpec((4, 512, 384), lambda i, w: (0, 0, 0)),
            pl.BlockSpec((128, 512), lambda i, w: (0, w[i])),
        ],
        scratch_shapes=[
            pltpu.VMEM((512, 1536), F32),
            pltpu.VMEM((512, 1), F32),
            pltpu.VMEM((512, 512), F32),
        ],
    )
    return pl.pallas_call(
        qkv_kernel,
        grid_spec=grid_spec,
        out_shape=[
            jax.ShapeDtypeStruct((4, 512, 384), BF16),
            jax.ShapeDtypeStruct((128, 4096), F32),
        ],
        name="qkv_heads",
    )(where, own, oth, hot, base, gain, proj, cosine, sine)


def attend_kernel(slot_ref, x0_ref, x1_ref, x2_ref, x3_ref, out_ref, q_ref, k_ref, v_ref):
    for rel, x_ref in enumerate((x0_ref, x1_ref, x2_ref, x3_ref)):
        for half in range(2):
            base = pl.multiple_of(slot_ref[2 * rel + half] * 256, 256)
            rows = slice(256 * half, 256 * half + 256)
            q_ref[pl.ds(base, 256), :] = x_ref[rows, 0:128]
            k_ref[pl.ds(base, 256), :] = x_ref[rows, 128:256]
            v_ref[pl.ds(base, 256), :] = x_ref[rows, 256:384]
    row = lax.broadcasted_iota(jnp.int32, (256, 256), 0)
    lane = lax.broadcasted_iota(jnp.int32, (256, 256), 1)
    causal = lane <= row
    scale = HD ** (-0.5)
    for block in range(8):
        width = 256 * block + 256
        query = q_ref[256 * block : width, :]
        scores = lax.dot_general(
            query, k_ref[0:width, :], (((1,), (1,)), ((), ())), preferred_element_type=F32
        )
        last = jnp.where(causal, scores[:, width - 256 :], NEG_FILL)
        if block > 0:
            scores = jnp.concatenate([scores[:, : width - 256], last], axis=1)
        else:
            scores = last
        top = jnp.max(scores, axis=1, keepdims=True)
        weights = jnp.exp((scores - top) * scale)
        total = jnp.sum(weights, axis=1, keepdims=True)
        mixed = dot32(weights.astype(BF16), v_ref[0:width, :])
        base = pl.multiple_of(slot_ref[8 + block] * 256, 256)
        out_ref[pl.ds(base, 256), :] = (mixed / total).astype(BF16)


def attend(slots, pieces):
    return pl.pallas_call(
        attend_kernel,
        in_specs=[SM] + [VM] * 4,
        out_specs=VM,
        out_shape=jax.ShapeDtypeStruct((2048, 128), BF16),
        scratch_shapes=[pltpu.VMEM((2048, 128), BF16)] * 3,
        name="attend",
    )(slots, *pieces)


def out_kernel(where_ref, own_ref, oth_ref, home_ref, *refs):
    parts, (own_out_ref, oth_out_ref, left_ref) = refs[:9], refs[9:]
    for side, src_ref in enumerate((own_ref, oth_ref)):
        for far in range(4):
            for rel in range(4):
                head = where_ref[4 + far] * 4 + where_ref[8 + rel]
                lane = pl.multiple_of(head * 128, 128)
                at = 512 * far + 128 * rel
                left_ref[128 * side : 128 * side + 128, pl.ds(lane, 128)] = src_ref[
                    :, at : at + 128
                ]

    def left(unit):
        return left_ref[:, pl.ds(pl.multiple_of(where_ref[unit] * 512, 512), 512)]

    for quarter in range(4):
        near = quarter < 2
        half = where_ref[12] if near else 1 - where_ref[12]
        lane = pl.multiple_of(half * 1024 + (quarter % 2) * 512, 512)
        total = dot32(left(0), home_ref[:, pl.ds(lane, 512)])
        for unit in range(3):
            block, side_x, side_y = parts[3 * unit : 3 * unit + 3]
            if near:
                right = block[:, 512 * quarter : 512 * quarter + 512]
            else:
                right = (side_x, side_y)[quarter - 2][...]
            total += dot32(left(unit + 1), right)
        own_out_ref[:, pl.ds(lane, 512)] = total[:128]
        oth_out_ref[:, pl.ds(lane, 512)] = total[128:].astype(oth_out_ref.dtype)


def out_branches(where, own, oth, home, parts):
    return pl.pallas_call(
        out_kernel,
        in_specs=[SM] + [VM] * (3 + len(parts)),
        out_specs=[VM, VM],
        out_shape=[
            jax.ShapeDtypeStruct((128, 2048), F32),
            jax.ShapeDtypeStruct((128, 2048), BF16),
        ],
        scratch_shapes=[pltpu.VMEM((256, 2048), BF16)],
        name="out_branch",
    )(where, own, oth, home, *parts)


def block_body(
    ids,
    block_order,
    embed,
    mix_gain,
    in_proj,
    short_filter,
    long_filter,
    conv_skip,
    hyena_out,
    attn_gain,
    qkv_proj,
    attn_out,
):
    half_at = lax.axis_index("dp")
    ctx = lax.axis_index("context")
    plane = lax.axis_index("tensor")
    edge = jnp.logical_or(plane == 0, plane == 3)
    order = block_order.astype(jnp.int32)
    half_lane = half_at * 2048

    home = rows_of(hyena_out, half_lane, 2048)
    units = along_chain(rows_of(hyena_out, half_lane + ctx * 512, 512), edge)
    parts = []
    for unit in units:
        side_x = swap_axis(unit, "context", 1)
        side_y = swap_axis(unit, "context", 2)
        corner_top = swap_axis(side_y[:256], "context", 1)
        corner_low = swap_axis(side_x[256:], "context", 2)
        parts += [unit, side_x, side_y, corner_top, corner_low]

    all_ids = lax.all_to_all(
        jnp.tile(ids[None], (16, 1)), ("context", "tensor"), 0, 0, tiled=True
    ).reshape(8, 256)

    base = jnp.concatenate([embed[code : code + 1] for code in CODES], axis=0)
    mixed_in = rms_scale(base, mix_gain)
    table = jnp.einsum(
        "rd,jdc->jrc", mixed_in, in_proj, preferred_element_type=F32
    ).astype(BF16)
    packed = jnp.concatenate(
        [
            table.astype(F32).reshape(12, 512),
            short_filter.reshape(9, 512),
            conv_skip.reshape(1, 512),
            long_filter.reshape(8, 512),
        ],
        axis=0,
    )
    everything = lax.all_to_all(
        jnp.tile(packed[None], (4, 1, 1)), "tensor", 0, 0, tiled=True
    )
    tables = everything[:, :12].reshape(4, 3, 1, 4, 512)
    shorts = everything[:, 12:21].reshape(4, 3, 3, 1, 512)
    coef = (tables * shorts).transpose(1, 0, 4, 2, 3).reshape(3, 2048, 12)
    coarse = lax.reduce_precision(coef, 8, 7)
    coef = jnp.concatenate([coarse, coef - coarse], axis=2).astype(BF16)
    skip = everything[:, 21].reshape(2048, 1)
    taps = everything[:, 22:].reshape(128, 128)

    slot_pair = 2 * ctx + jnp.arange(2, dtype=jnp.int32)
    slot_ids = jnp.arange(8, dtype=jnp.int32)
    own_hit = slot_ids[None, :] == slot_pair[:, None]
    owned = jnp.sum(jnp.where(own_hit, order[None, :], 0), axis=1)
    before_hit = order[None, :] == owned[:, None] - 1
    own_ids = jnp.sum(jnp.where(own_hit[:, :, None], all_ids[None], 0), axis=1)
    before_ids = jnp.sum(jnp.where(before_hit[:, :, None], all_ids[None], 0), axis=1)
    span = jnp.concatenate([before_ids, own_ids], axis=1)
    codes = jnp.array(CODES, jnp.int32)
    hot = jnp.stack(
        [
            (span[None, :, 128 - lag : 512 - lag] == codes[:, None, None]).astype(BF16)
            for lag in range(3)
        ]
    ).reshape(12, 768)
    hot = jnp.concatenate([hot, hot], axis=0)
    own_mix = hyena_mixes(coef, hot, taps, skip)
    oth_mix = swap_axis(own_mix, "dp", 1)

    unit_plane = [
        jnp.array([1, 0, 3, 2], jnp.int32)[plane],
        jnp.array([2, 2, 1, 1], jnp.int32)[plane],
        jnp.array([3, 3, 0, 0], jnp.int32)[plane],
    ]
    where = jnp.stack([plane] + unit_plane + [ctx ^ rel for rel in range(4)])
    own_half, give_half = hyena_branches(where, own_mix, oth_mix, home, parts)
    got_half = swap_axis(give_half, "dp", 1)

    local_pos = (
        owned[:, None] * 256 + jnp.arange(256, dtype=jnp.int32)[None, :]
    ).reshape(512)
    inverse_freq = THETA ** (-(2.0 * jnp.arange(64, dtype=F32)) / HD)
    angles = local_pos.astype(F32)[:, None] * inverse_freq[None, :]
    cosine = jnp.cos(angles)
    sine = jnp.sin(angles)
    cosine = jnp.concatenate([cosine, cosine], axis=1)
    sine = jnp.concatenate([-sine, sine], axis=1)
    own_hot = (own_ids.reshape(512, 1) == codes[None, :]).astype(BF16)
    blocks = [half_at * 4 + at for at in range(4)] + [(1 - half_at) * 4 + at for at in range(4)]
    where = jnp.stack(blocks + [plane] + [ctx ^ rel for rel in range(4)])
    heads, stream_rows = qkv_heads(
        where, own_half, got_half, own_hot, base, attn_gain[None], qkv_proj, cosine, sine
    )

    pieces = [heads[0]] + [swap_axis(heads[rel], "context", rel) for rel in range(1, 4)]
    near_slots = jnp.stack([2 * (ctx ^ rel) + half for rel in range(4) for half in range(2)])
    hit = near_slots[:, None] == slot_ids[None, :]
    place = jnp.sum(jnp.where(hit, order[None, :], 0), axis=1)
    holder = jnp.sum(
        jnp.where(place[None, :] == slot_ids[:, None], slot_ids[None, :], 0), axis=1
    )
    attended = attend(jnp.concatenate([place, holder]), pieces).reshape(4, 512, 128)
    mine = jnp.concatenate(
        [attended[0]] + [swap_axis(attended[rel], "context", rel) for rel in range(1, 4)],
        axis=1,
    ).reshape(4, 128, 512)

    def rows_for(rel):
        return lax.dynamic_index_in_dim(mine, plane ^ rel, 0, keepdims=False)

    own_att = jnp.concatenate(
        [rows_for(0)] + [swap_axis(rows_for(rel), "tensor", rel) for rel in range(1, 4)],
        axis=1,
    )
    oth_att = swap_axis(own_att, "dp", 1)

    home = rows_of(attn_out, half_lane, 2048)
    cross = (ctx & 1) ^ (ctx >> 1)
    units = along_chain(rows_of(attn_out, half_lane + cross * 1024, 1024), edge)
    parts = []
    for unit in units:
        parts += [
            unit,
            swap_axis(unit[:, :512], "context", 1),
            swap_axis(unit[:, 512:], "context", 2),
        ]
    where = jnp.stack(
        [plane]
        + unit_plane
        + [plane ^ rel for rel in range(4)]
        + [ctx ^ rel for rel in range(4)]
        + [cross]
    )
    own_out, give_out = out_branches(where, own_att, oth_att, home, parts)
    got_out = swap_axis(give_out, "dp", 1).astype(F32)
    first = half_at == 0
    attn_rows = jnp.concatenate(
        [jnp.where(first, own_out, got_out), jnp.where(first, got_out, own_out)], axis=1
    )
    return stream_rows + attn_rows


def solution(mesh):
    grid_shape = dict(mesh.shape)
    square = (grid_shape["dp"], grid_shape["context"], grid_shape["tensor"]) == (2, 4, 4)
    body = block_body if square else generic_body
    placed = (
        P(("dp", "context", "tensor")),
        P("dp"),
        P(),
        P(),
        P(None, None, "tensor"),
        P(None, None, "tensor"),
        P("tensor", None),
        P("tensor"),
        P("tensor", None),
        P(),
        P(None, None, "tensor"),
        P("tensor", None),
    )
    return jax.shard_map(
        body,
        mesh=mesh,
        in_specs=placed,
        out_specs=P(("dp", "context", "tensor"), None),
        check_vma=False,
    )
```

```python
import functools
import math

import jax
import jax.numpy as jnp
import numpy as np
from jax import lax
from jax.experimental import pallas as pl
from jax.experimental.pallas import tpu as pltpu
from jax.sharding import PartitionSpec as P

HD = 128
GROUP_CH = 16


EPS = 1e-06
THETA = 1000000.0
NEG_FILL = -1e30


def rms_scale(row_data, gain_vec):
    values = row_data.astype(jnp.float32)
    factor = lax.rsqrt(jnp.mean(values * values, axis=-1, keepdims=True) + EPS)
    return (values * factor * gain_vec).astype(jnp.bfloat16)


def toeplitz(long_filter):
    filter_len = long_filter.shape[1]
    tap_lag = (
        jnp.arange(filter_len, dtype=jnp.int32)[:, None]
        - jnp.arange(filter_len, dtype=jnp.int32)[None, :]
    )
    near_taps = jnp.take(long_filter, jnp.clip(tap_lag, 0, filter_len - 1), axis=1)
    far_taps = jnp.take(long_filter, jnp.clip(tap_lag + filter_len, 0, filter_len - 1), axis=1)
    near_taps = jnp.where(tap_lag[None] >= 0, near_taps, jnp.zeros_like(near_taps))
    far_taps = jnp.where(tap_lag[None] < 0, far_taps, jnp.zeros_like(far_taps))
    return (near_taps, far_taps)


def long_conv(padded, long_filter, group_width):
    filter_len = long_filter.shape[1]
    near_taps, far_taps = toeplitz(long_filter)
    row_total = padded.shape[0]
    chan_total = padded.shape[1]
    blocks = padded.reshape(
        row_total // filter_len, filter_len, chan_total // group_width, group_width
    )
    current_part = jnp.einsum(
        "grs,bsgc->brgc", near_taps, blocks[1:], precision=lax.Precision.HIGHEST
    )
    before = jnp.einsum("grs,bsgc->brgc", far_taps, blocks[:-1], precision=lax.Precision.HIGHEST)
    return (current_part + before).reshape(row_total - filter_len, chan_total)


def short_conv(padded_rows, short_filter, out_len):
    taps = short_filter.shape[1]
    result = jnp.zeros((padded_rows.shape[0], out_len, padded_rows.shape[2]), jnp.float32)
    for tap_at in range(taps):
        offset = taps - 1 - tap_at
        result = (
            result + short_filter[:, tap_at][:, None, :] * padded_rows[:, offset : offset + out_len]
        )
    return result


def rotate(values, positions, head_dim):
    half_dim = head_dim // 2
    inverse_freq = THETA ** (-(2.0 * jnp.arange(half_dim, dtype=jnp.float32)) / head_dim)
    angles = positions.astype(jnp.float32)[:, None] * inverse_freq[None, :]
    cosine_part = jnp.cos(angles)[:, None, :]
    sine_part = jnp.sin(angles)[:, None, :]
    lower_half = values[..., :half_dim]
    upper_half = values[..., half_dim:]
    return jnp.concatenate(
        [
            lower_half * cosine_part - upper_half * sine_part,
            upper_half * cosine_part + lower_half * sine_part,
        ],
        axis=-1,
    )


def generic_body(
    ids,
    block_order,
    embed,
    mix_gain,
    in_proj,
    short_filter,
    long_filter,
    conv_skip,
    hyena_out,
    attn_gain,
    qkv_proj,
    attn_out,
):
    tok_rows = ids.shape[0]
    tensor_count = lax.axis_size("tensor")
    context_count = lax.axis_size("context")
    ctx_rows = tok_rows * tensor_count
    block_rows = ctx_rows // 2
    filter_len = long_filter.shape[1]
    short_len = short_filter.shape[1]
    halo_len = filter_len + short_len - 2
    chan_local = in_proj.shape[2]
    context_at = lax.axis_index("context")
    vocab_ids = jnp.arange(embed.shape[0], dtype=jnp.int32)
    chosen = (ids[:, None] == vocab_ids[None, :]).astype(jnp.bfloat16)
    embedded = jnp.dot(chosen, embed, preferred_element_type=jnp.float32).astype(jnp.bfloat16)
    embedded_all = lax.all_gather(embedded, "tensor", axis=0, tiled=True)
    mixed_in = rms_scale(embedded_all, mix_gain)
    projected = jnp.einsum(
        "rd,jdc->jrc", mixed_in, in_proj, preferred_element_type=jnp.float32
    ).astype(jnp.bfloat16)
    slot_ids = jnp.arange(2 * context_count, dtype=jnp.int32)
    slot_pair = 2 * context_at + jnp.arange(2, dtype=jnp.int32)
    owned_blocks = jnp.sum(
        jnp.where(slot_ids[None, :] == slot_pair[:, None], block_order[None, :], 0), axis=1
    )
    local_pos = (
        owned_blocks[:, None] * block_rows + jnp.arange(block_rows, dtype=jnp.int32)[None, :]
    ).reshape(ctx_rows)
    tail_rows = jnp.stack(
        [projected[:, block_rows - halo_len : block_rows], projected[:, ctx_rows - halo_len :]]
    )
    all_tails = lax.all_gather(tail_rows, "context", axis=0, tiled=True)
    out_len = filter_len - 1 + block_rows
    pieces = []
    for block_at in range(2):
        holder_hit = (block_order == owned_blocks[block_at] - 1).astype(jnp.bfloat16)
        before_rows = jnp.einsum(
            "s,sjrc->jrc", holder_hit, all_tails, preferred_element_type=jnp.float32
        )
        own_rows = projected[:, block_at * block_rows : (block_at + 1) * block_rows].astype(
            jnp.float32
        )
        extended = jnp.concatenate([before_rows, own_rows], axis=1)
        filtered = short_conv(extended, short_filter, out_len)
        gated_rows = filtered[1] * filtered[2]
        padded = jnp.concatenate([jnp.zeros((1, chan_local), jnp.float32), gated_rows], axis=0)
        long_mix = long_conv(padded, long_filter, GROUP_CH)
        own_gate = gated_rows[filter_len - 1 :]
        pieces.append(
            (filtered[0, filter_len - 1 :] * (long_mix + conv_skip * own_gate)).astype(jnp.bfloat16)
        )
    hyena_mix = jnp.concatenate(pieces, axis=0)
    hyena_own = lax.psum_scatter(
        jnp.dot(hyena_mix, hyena_out, preferred_element_type=jnp.float32),
        "tensor",
        scatter_dimension=0,
        tiled=True,
    )
    stream_own = embedded.astype(jnp.float32) + hyena_own
    stream_all = lax.all_gather(stream_own, "tensor", axis=0, tiled=True)
    attn_in = rms_scale(stream_all, attn_gain)
    projections = jnp.einsum("rd,jdf->jrf", attn_in, qkv_proj, preferred_element_type=jnp.float32)
    local_heads = projections.shape[2] // HD
    shaped = projections.reshape(3, ctx_rows, local_heads, HD)
    queries = rotate(shaped[0], local_pos, HD).astype(jnp.bfloat16)
    keys_flat = (
        rotate(shaped[1], local_pos, HD).astype(jnp.bfloat16).reshape(ctx_rows, local_heads * HD)
    )
    values_flat = shaped[2].astype(jnp.bfloat16).reshape(ctx_rows, local_heads * HD)
    score_scale = HD ** (-0.5)
    start_state = (
        jnp.full((2, block_rows, local_heads), NEG_FILL, jnp.float32),
        jnp.zeros((2, block_rows, local_heads), jnp.float32),
        jnp.zeros((2, block_rows, local_heads, HD), jnp.float32),
    )
    key_piece = lax.all_gather(keys_flat, "context", axis=0, tiled=True)
    value_piece = lax.all_gather(values_flat, "context", axis=0, tiled=True)
    piece_len = key_piece.shape[0]
    sub_len = math.gcd(piece_len, 512)

    def attend_sub(sub_index, carried):
        key_block = lax.dynamic_slice_in_dim(key_piece, sub_index * sub_len, sub_len, 0).reshape(
            sub_len, local_heads, HD
        )
        value_block = lax.dynamic_slice_in_dim(
            value_piece, sub_index * sub_len, sub_len, 0
        ).reshape(sub_len, local_heads, HD)
        row_ids = sub_index * sub_len + jnp.arange(sub_len, dtype=jnp.int32)
        holder = row_ids // block_rows
        key_pos = (
            jnp.sum(
                jnp.where(holder[:, None] == slot_ids[None, :], block_order[None, :], 0), axis=1
            )
            * block_rows
            + row_ids % block_rows
        )
        top_all, sums_all, weighted_all = carried
        outputs = []
        for block_at in range(2):
            query_rows = queries[block_at * block_rows : (block_at + 1) * block_rows]
            query_pos = local_pos[block_at * block_rows : (block_at + 1) * block_rows]
            top_score = top_all[block_at]
            weight_sum = sums_all[block_at]
            weighted = weighted_all[block_at]
            scores = (
                jnp.einsum(
                    "qhd,khd->qhk", query_rows, key_block, preferred_element_type=jnp.float32
                )
                * score_scale
            )
            visible = key_pos[None, None, :] <= query_pos[:, None, None]
            scores = jnp.where(visible, scores, NEG_FILL)
            new_top = jnp.maximum(top_score, jnp.max(scores, axis=-1))
            rescale = jnp.exp(top_score - new_top)
            weights = jnp.where(visible, jnp.exp(scores - new_top[..., None]), 0.0)
            weight_sum = weight_sum * rescale + jnp.sum(weights, axis=-1)
            weighted = weighted * rescale[..., None] + jnp.einsum(
                "qhk,khd->qhd",
                weights.astype(jnp.bfloat16),
                value_block,
                preferred_element_type=jnp.float32,
            )
            result = (new_top, weight_sum, weighted)
            outputs.append(result)
        return tuple((jnp.stack([entry[field] for entry in outputs]) for field in range(3)))

    _, sums_final, weighted_final = lax.fori_loop(0, piece_len // sub_len, attend_sub, start_state)
    attended = (
        (weighted_final / sums_final[..., None])
        .astype(jnp.bfloat16)
        .reshape(ctx_rows, local_heads * HD)
    )
    attn_own = lax.psum_scatter(
        jnp.dot(attended, attn_out, preferred_element_type=jnp.float32).astype(jnp.bfloat16),
        "tensor",
        scatter_dimension=0,
        tiled=True,
    ).astype(jnp.float32)
    return stream_own + attn_own


CODES = (65, 67, 71, 84)
BF16 = jnp.bfloat16
F32 = jnp.float32
VM = pl.BlockSpec(memory_space=pltpu.VMEM)
SM = pl.BlockSpec(memory_space=pltpu.SMEM)

UNIT, CTX, PLANE, CROSS, HALF, OTHER = 0, 4, 8, 12, 13, 14
MINE, THEIRS, SLOTS = 15, 17, 19


def position_table():
    rows = []
    for half in range(2):
        for ctx in range(4):
            for plane in range(4):
                units = [plane, (1, 0, 3, 2)[plane], (2, 2, 1, 1)[plane], (3, 3, 0, 0)[plane]]
                row = units + [ctx ^ rel for rel in range(4)] + [plane ^ rel for rel in range(4)]
                row += [(ctx & 1) ^ (ctx >> 1), half, 1 - half]
                row += [2 * half, 2 * half + 1, 2 - 2 * half, 3 - 2 * half]
                row += [2 * (ctx ^ rel) + at for rel in range(4) for at in range(2)]
                rows.append(row)
    return np.array(rows, np.int32)


def swap(value, axis, mask):
    size = lax.axis_size(axis)
    return lax.ppermute(value, axis, [(at, at ^ mask) for at in range(size)])


def rows_of(weights, lane_start, width):
    return lax.dynamic_slice(weights, (0, lane_start), (weights.shape[0], width))


def along_chain(piece, edge_plane):
    middle = [(1, 2), (2, 1)]
    outward = [(1, 0), (2, 3)]
    near = swap(piece, "tensor", 1)
    across = lax.ppermute(piece, "tensor", middle)
    far_mid = lax.ppermute(near, "tensor", middle)
    across_out = lax.ppermute(across, "tensor", outward)
    far_out = lax.ppermute(far_mid, "tensor", outward)
    return (
        near,
        jnp.where(edge_plane, across_out, across),
        jnp.where(edge_plane, far_out, far_mid),
    )


def dot32(left, right):
    return jnp.dot(left, right, preferred_element_type=F32)


def hyena_kernel(where_ref, coef_ref, hot_ref, taps_ref, skip_ref, mix_ref):
    hot = hot_ref[...]
    first, second, third = (dot32(coef_ref[j], hot) for j in range(3))
    gated = second * third
    packed = gated.astype(BF16)
    row = lax.broadcasted_iota(jnp.int32, (128, 128), 0)
    lane = lax.broadcasted_iota(jnp.int32, (128, 128), 1)
    near = lane >= row
    mixed = []
    for group in range(16):
        spread = jnp.broadcast_to(taps_ref[group : group + 1, :], (128, 128))
        rolled = pltpu.roll(spread, 0, 1, stride=1, stride_axis=0)
        zero = jnp.zeros_like(rolled)
        matrix = jnp.concatenate(
            [jnp.where(near, zero, rolled), jnp.where(near, rolled, zero)], axis=0
        ).astype(BF16)
        chans = packed[16 * group : 16 * group + 16]
        left = jnp.concatenate(
            [chans[:, at : at + 256] for at in (0, 128, 384, 512)], axis=0
        )
        result = dot32(left, matrix)
        mixed.append(jnp.concatenate([result[16 * i : 16 * i + 16] for i in range(4)], axis=1))
    long_mix = jnp.concatenate(mixed, axis=0)
    own_gate = jnp.concatenate([gated[:, 128:384], gated[:, 512:768]], axis=1)
    own_first = jnp.concatenate([first[:, 128:384], first[:, 512:768]], axis=1)
    mix = own_first * (long_mix + skip_ref[...] * own_gate)
    mix_ref[...] = mix.T.astype(BF16)


def hyena_mixes(where, coef, hot, taps, skip):
    chans = coef.shape[1]
    step = 256
    return pl.pallas_call(
        hyena_kernel,
        grid_spec=pltpu.PrefetchScalarGridSpec(
            num_scalar_prefetch=1,
            grid=(chans // step,),
            in_specs=[
                pl.BlockSpec((3, step, coef.shape[2]), lambda i, w: (0, i, 0)),
                pl.BlockSpec(hot.shape, lambda i, w: (0, 0)),
                pl.BlockSpec((step // 16, 128), lambda i, w: (i, 0)),
                pl.BlockSpec((step, 1), lambda i, w: (i, 0)),
            ],
            out_specs=pl.BlockSpec(
                (512, step), lambda i, w: (0, w[PLANE + i // 2] * 2 + i % 2)
            ),
        ),
        out_shape=jax.ShapeDtypeStruct((512, chans), BF16),
        name="hyena_mix",
    )(where, coef, hot, taps, skip)


def both(own_ref, oth_ref):
    return jnp.concatenate([own_ref[...], oth_ref[...]], axis=0)


def branch_lane(where_ref, rel):
    return pl.ds(pl.multiple_of(where_ref[CTX + rel] * 512, 512), 512)


def branch_a_kernel(where_ref, own0, oth0, own1, oth1, own2, oth2, home_ref, *refs):
    block1, block2, sum_ref = refs[:4], refs[4:8], refs[8]
    left0, left1, left2 = both(own0, oth0), both(own1, oth1), both(own2, oth2)
    rows = own0.shape[0]
    for rel in range(4):
        lane = branch_lane(where_ref, rel)
        total = dot32(left0, home_ref[:, lane]) + dot32(left1, block1[rel][...])
        total += dot32(left2, block2[rel][...])
        sum_ref[0, :, lane] = total[:rows]
        sum_ref[1, :, lane] = total[rows:]


def branch_b_kernel(where_ref, own3, oth3, sum_ref, *refs):
    block3, (own_ref, oth_ref) = refs[:4], refs[4:]
    left3 = both(own3, oth3)
    rows = own3.shape[0]
    for rel in range(4):
        lane = branch_lane(where_ref, rel)
        total = dot32(left3, block3[rel][...])
        own_ref[:, lane] = sum_ref[0, :, lane] + total[:rows]
        oth_ref[:, lane] = (sum_ref[1, :, lane] + total[rows:]).astype(BF16)


def hyena_branches(where, own_mix, oth_mix, home, parts):
    tile = 256
    grid = (512 // tile,)

    def mixes(at):
        return [pl.BlockSpec((tile, 512), lambda i, w: (i, w[UNIT + at]))] * 2

    sums = pl.BlockSpec((2, tile, 2048), lambda i, w: (0, i, 0))
    flat = pl.BlockSpec((tile, 2048), lambda i, w: (i, 0))
    sum_shape = jax.ShapeDtypeStruct((2, 512, 2048), F32)
    half_shapes = [
        jax.ShapeDtypeStruct((512, 2048), F32),
        jax.ShapeDtypeStruct((512, 2048), BF16),
    ]

    def call(kernel, in_specs, out_specs, out_shape, operands):
        return pl.pallas_call(
            kernel,
            grid_spec=pltpu.PrefetchScalarGridSpec(
                num_scalar_prefetch=1, grid=grid, in_specs=in_specs, out_specs=out_specs
            ),
            out_shape=out_shape,
            name="hyena_branch",
        )(where, *operands)

    mix = [own_mix, oth_mix]
    home_spec = pl.BlockSpec((512, 2048), lambda i, w: (0, w[HALF]))
    partial = call(
        branch_a_kernel,
        mixes(0) + mixes(1) + mixes(2) + [home_spec] + [VM] * 8,
        sums,
        sum_shape,
        mix * 3 + [home] + parts[0] + parts[1],
    )
    return call(
        branch_b_kernel,
        mixes(3) + [sums] + [VM] * 4,
        [flat, flat],
        half_shapes,
        mix + [partial] + parts[2],
    )


def qkv_kernel(where_ref, half_ref, hot_ref, base_ref, gain_ref, proj_ref, *refs, first):
    at = pl.program_id(0)
    if first:
        total_ref, power_ref, rows_ref, block_ref = refs
    else:
        part_ref, part_power_ref, cos_ref, sin_ref = refs[:4]
        head_refs = refs[4:8]
        rows_ref, total_ref, power_ref, block_ref = refs[8:]

    @pl.when(at == 0)
    def _():
        if first:
            total_ref[...] = jnp.zeros_like(total_ref)
            power_ref[...] = jnp.zeros_like(power_ref)
        else:
            total_ref[...] = part_ref[...]
            power_ref[...] = part_power_ref[...]

    stream = dot32(hot_ref[...], base_ref[...]) + half_ref[...].astype(F32)
    block_ref[...] = stream
    rows_ref[...] = block_ref[pl.ds(pl.multiple_of(where_ref[PLANE] * 128, 128), 128), :]
    power_ref[...] += jnp.sum(stream * stream, axis=1, keepdims=True)
    scaled = (stream * gain_ref[...]).astype(BF16)
    for j in range(3):
        total_ref[:, 512 * j : 512 * j + 512] += dot32(scaled, proj_ref[j])
    if first:
        return

    @pl.when(at == 1)
    def _():
        factor = lax.rsqrt(power_ref[...] * (1.0 / 4096.0) + EPS)
        cosine = cos_ref[...] * factor
        sine = sin_ref[...] * factor
        for rel in range(4):
            for j in range(3):
                lane = pl.multiple_of(where_ref[CTX + rel] * 128 + 512 * j, 128)
                piece = total_ref[:, pl.ds(lane, 128)]
                if j < 2:
                    piece = piece * cosine + pltpu.roll(piece, 64, 1) * sine
                else:
                    piece = piece * factor
                head_refs[rel][:, 128 * j : 128 * j + 128] = piece.astype(BF16)


def qkv_half(where, half, hot, base, gain, proj, extra=()):
    first = not extra
    at = MINE if first else THEIRS
    whole = lambda shape: pl.BlockSpec(shape, lambda i, w: (0,) * len(shape))
    in_specs = [
        pl.BlockSpec((512, 1024), lambda i, w: (0, i)),
        whole(hot.shape),
        pl.BlockSpec((base.shape[0], 1024), lambda i, w: (0, w[at + i])),
        pl.BlockSpec((1, 1024), lambda i, w: (0, w[at + i])),
        pl.BlockSpec((3, 1024, 512), lambda i, w: (0, w[at + i], 0)),
    ]
    rows_spec = pl.BlockSpec((128, 1024), lambda i, w: (0, i))
    rows_shape = jax.ShapeDtypeStruct((128, 2048), F32)
    scratch = [pltpu.VMEM((512, 1024), F32)]
    if first:
        out_specs = [whole((512, 1536)), whole((512, 1)), rows_spec]
        out_shape = [
            jax.ShapeDtypeStruct((512, 1536), F32),
            jax.ShapeDtypeStruct((512, 1), F32),
            rows_shape,
        ]
    else:
        in_specs += [whole(value.shape) for value in extra]
        out_specs = [whole((512, 384))] * 4 + [rows_spec]
        out_shape = [jax.ShapeDtypeStruct((512, 384), BF16)] * 4 + [rows_shape]
        scratch = [pltpu.VMEM((512, 1536), F32), pltpu.VMEM((512, 1), F32)] + scratch
    return pl.pallas_call(
        functools.partial(qkv_kernel, first=first),
        grid_spec=pltpu.PrefetchScalarGridSpec(
            num_scalar_prefetch=1,
            grid=(2,),
            in_specs=in_specs,
            out_specs=out_specs,
            scratch_shapes=scratch,
        ),
        out_shape=out_shape,
        name="qkv_half",
    )(where, half, hot, base, gain, proj, *extra)


def attend_kernel(slot_ref, *refs):
    x_refs, out_refs, (q_ref, k_ref, v_ref, mixed_ref) = refs[:4], refs[4:8], refs[8:]
    for rel, x_ref in enumerate(x_refs):
        for half in range(2):
            base = pl.multiple_of(slot_ref[2 * rel + half] * 256, 256)
            rows = slice(256 * half, 256 * half + 256)
            q_ref[pl.ds(base, 256), :] = x_ref[rows, 0:128]
            k_ref[pl.ds(base, 256), :] = x_ref[rows, 128:256]
            v_ref[pl.ds(base, 256), :] = x_ref[rows, 256:384]
    row = lax.broadcasted_iota(jnp.int32, (256, 256), 0)
    lane = lax.broadcasted_iota(jnp.int32, (256, 256), 1)
    causal = lane <= row
    scale = HD ** (-0.5)
    for block in range(8):
        width = 256 * block + 256
        query = q_ref[256 * block : width, :]
        scores = lax.dot_general(
            query, k_ref[0:width, :], (((1,), (1,)), ((), ())), preferred_element_type=F32
        )
        last = jnp.where(causal, scores[:, width - 256 :], NEG_FILL)
        if block > 0:
            scores = jnp.concatenate([scores[:, : width - 256], last], axis=1)
        else:
            scores = last
        top = jnp.max(scores, axis=1, keepdims=True)
        weights = jnp.exp((scores - top) * scale)
        total = jnp.sum(weights, axis=1, keepdims=True)
        mixed = dot32(weights.astype(BF16), v_ref[0:width, :])
        mixed_ref[256 * block : width, :] = (mixed / total).astype(BF16)
    for rel, out_ref in enumerate(out_refs):
        for half in range(2):
            base = pl.multiple_of(slot_ref[2 * rel + half] * 256, 256)
            out_ref[256 * half : 256 * half + 256, :] = mixed_ref[pl.ds(base, 256), :]


def attend(slots, pieces):
    return pl.pallas_call(
        attend_kernel,
        in_specs=[SM] + [VM] * 4,
        out_specs=[VM] * 4,
        out_shape=[jax.ShapeDtypeStruct((512, 128), BF16)] * 4,
        scratch_shapes=[pltpu.VMEM((2048, 128), BF16)] * 4,
        name="attend",
    )(slots, *pieces)


def out_kernel(where_ref, own_ref, oth_ref, rows_ref, home_ref, *refs):
    parts, refs = refs[:9], refs[9:]
    own_out_ref, oth_out_ref, left_ref, home_vm, *rest = refs
    held, sem = rest[:9], rest[9]
    lane = pl.multiple_of(where_ref[HALF] * 2048, 2048)
    copies = [pltpu.make_async_copy(home_ref.at[:, pl.ds(lane, 2048)], home_vm, sem.at[9])]
    copies += [
        pltpu.make_async_copy(part, room, sem.at[at])
        for at, (part, room) in enumerate(zip(parts, held))
    ]
    copies[0].start()
    for kind in range(3):
        for unit in range(3):
            copies[1 + 3 * unit + kind].start()
    for side, src_ref in enumerate((own_ref, oth_ref)):
        for far in range(4):
            for rel in range(4):
                head = where_ref[PLANE + far] * 4 + where_ref[CTX + rel]
                lane = pl.multiple_of(head * 128, 128)
                at = 512 * far + 128 * rel
                left_ref[128 * side : 128 * side + 128, pl.ds(lane, 128)] = src_ref[
                    :, at : at + 128
                ]

    def left(unit):
        return left_ref[:, pl.ds(pl.multiple_of(where_ref[UNIT + unit] * 512, 512), 512)]

    lanes = []
    copies[0].wait()
    for quarter in range(4):
        half = where_ref[CROSS] if quarter < 2 else 1 - where_ref[CROSS]
        lanes.append(pl.multiple_of(half * 1024 + (quarter % 2) * 512, 512))
        own_out_ref[:, pl.ds(lanes[quarter], 512)] = rows_ref[:, pl.ds(lanes[quarter], 512)]
    for quarter in range(4):
        for unit in range(3):
            if quarter != 1:
                copies[1 + 3 * unit + max(quarter - 1, 0)].wait()
        total = dot32(left(0), home_vm[:, pl.ds(lanes[quarter], 512)])
        for unit in range(3):
            block, side_x, side_y = held[3 * unit : 3 * unit + 3]
            if quarter < 2:
                right = block[:, 512 * quarter : 512 * quarter + 512]
            else:
                right = (side_x, side_y)[quarter - 2][...]
            total += dot32(left(unit + 1), right)
        own_out_ref[:, pl.ds(lanes[quarter], 512)] += total[:128]
        oth_out_ref[:, pl.ds(lanes[quarter], 512)] = total[128:].astype(oth_out_ref.dtype)


def out_branches(where, own, oth, rows, home, parts):
    anywhere = pl.BlockSpec(memory_space=pl.ANY)
    flat = pl.BlockSpec((128, 2048), lambda i, w: (0, 0))
    return pl.pallas_call(
        out_kernel,
        grid_spec=pltpu.PrefetchScalarGridSpec(
            num_scalar_prefetch=1,
            grid=(1,),
            in_specs=[flat, flat, flat] + [anywhere] * (1 + len(parts)),
            out_specs=[pl.BlockSpec((128, 2048), lambda i, w: (0, w[HALF])), flat],
            scratch_shapes=[pltpu.VMEM((256, 2048), BF16), pltpu.VMEM((512, 2048), BF16)]
            + [pltpu.VMEM(part.shape, BF16) for part in parts]
            + [pltpu.SemaphoreType.DMA((10,))],
        ),
        out_shape=[jax.ShapeDtypeStruct((128, 4096), F32), jax.ShapeDtypeStruct((128, 2048), BF16)],
        name="out_branch",
    )(where, own, oth, rows, home, *parts)


def join_kernel(where_ref, own_any, rows_ref, got_ref, out_ref):
    out_ref[...] = rows_ref[...] + got_ref[...].astype(F32)


def join_halves(where, own, rows, got):
    piece = pl.BlockSpec((128, 1024), lambda i, w: (0, i))
    return pl.pallas_call(
        join_kernel,
        grid_spec=pltpu.PrefetchScalarGridSpec(
            num_scalar_prefetch=1,
            grid=(2,),
            in_specs=[pl.BlockSpec(memory_space=pl.ANY), piece, piece],
            out_specs=pl.BlockSpec((128, 1024), lambda i, w: (0, w[OTHER] * 2 + i)),
        ),
        out_shape=jax.ShapeDtypeStruct((128, 4096), F32),
        input_output_aliases={1: 0},
        name="join_halves",
    )(where, own, rows, got)


def block_body(*operands):
    return block_rows_out(*operands)


def block_rows_out(
    ids,
    block_order,
    embed,
    mix_gain,
    in_proj,
    short_filter,
    long_filter,
    conv_skip,
    hyena_out,
    attn_gain,
    qkv_proj,
    attn_out,
):
    half_at = lax.axis_index("dp")
    ctx = lax.axis_index("context")
    plane = lax.axis_index("tensor")
    edge = jnp.logical_or(plane == 0, plane == 3)
    order = block_order.astype(jnp.int32)
    half_lane = half_at * 2048
    table_rows = jnp.asarray(position_table())
    where = lax.dynamic_index_in_dim(
        table_rows, half_at * 16 + ctx * 4 + plane, 0, keepdims=False
    )

    piece = rows_of(hyena_out, half_lane + ctx * 512, 512)
    parts = []
    for unit in along_chain(piece, edge):
        parts.append(
            [unit, swap(unit, "context", 1), swap(unit, "context", 2), swap(unit, "context", 3)]
        )

    own_row = ids.astype(F32).reshape(1, 128)
    id_rows = jnp.concatenate(
        [own_row] + [swap(own_row, "context", rel) for rel in range(1, 4)], axis=1
    )

    base = jnp.concatenate([embed[code : code + 1] for code in CODES], axis=0)
    mixed_in = rms_scale(base, mix_gain)
    table = jnp.einsum(
        "rd,jdc->jrc", mixed_in, in_proj, preferred_element_type=F32
    ).astype(BF16)
    packed = jnp.concatenate(
        [
            table.astype(F32).reshape(12, 512),
            short_filter.reshape(9, 512),
            conv_skip.reshape(1, 512),
            long_filter.reshape(8, 512),
            id_rows,
        ],
        axis=0,
    )
    everything = jnp.stack([packed] + [swap(packed, "tensor", rel) for rel in range(1, 4)])
    slot_ids = jnp.arange(8, dtype=jnp.int32)
    place = jnp.sum(
        jnp.where(where[SLOTS : SLOTS + 8, None] == slot_ids[None, :], order[None, :], 0), axis=1
    )
    owned = place[:2]
    local_pos = (
        owned[:, None] * 256 + jnp.arange(256, dtype=jnp.int32)[None, :]
    ).reshape(512)
    inverse_freq = THETA ** (-(2.0 * jnp.arange(64, dtype=F32)) / HD)
    angles = local_pos.astype(F32)[:, None] * inverse_freq[None, :]
    cosine = jnp.cos(angles)
    sine = jnp.sin(angles)
    cosine = jnp.concatenate([cosine, cosine], axis=1)
    sine = jnp.concatenate([-sine, sine], axis=1)
    which = where[None, PLANE : PLANE + 4] == jnp.arange(4, dtype=jnp.int32)[:, None]
    plane_ids = everything[:, 30].reshape(1, 4, 4, 128)
    plane_ids = jnp.sum(jnp.where(which[:, :, None, None], plane_ids, 0.0), axis=1)
    all_ids = plane_ids.transpose(1, 0, 2).reshape(8, 256)
    tables = everything[:, :12].reshape(4, 3, 1, 4, 512)
    shorts = everything[:, 12:21].reshape(4, 3, 3, 1, 512)
    coef = (tables * shorts).transpose(1, 0, 4, 2, 3).reshape(3, 2048, 12)
    coarse = lax.reduce_precision(coef, 8, 7)
    coef = jnp.concatenate([coarse, coef - coarse], axis=2).astype(BF16)
    skip = everything[:, 21].reshape(2048, 1)
    taps = everything[:, 22:30].reshape(128, 128)

    before_hit = place[None, :] == owned[:, None] - 1
    own_ids = all_ids[:2]
    before_ids = jnp.sum(jnp.where(before_hit[:, :, None], all_ids[None], 0.0), axis=1)
    span = jnp.concatenate([before_ids, own_ids], axis=1)
    codes = jnp.array(CODES, F32)
    hot = jnp.stack(
        [
            (span[None, :, 128 - lag : 512 - lag] == codes[:, None, None]).astype(BF16)
            for lag in range(3)
        ]
    ).reshape(12, 768)
    hot = jnp.concatenate([hot, hot], axis=0)
    own_hot = (own_ids.reshape(512, 1) == codes[None, :]).astype(BF16)
    coef, hot, place, cosine, sine, own_hot, base = lax.optimization_barrier(
        (coef, hot, place, cosine, sine, own_hot, base)
    )

    own_mix = hyena_mixes(where, coef, hot, taps, skip)
    oth_mix = swap(own_mix, "dp", 1)

    own_half, give_half = hyena_branches(where, own_mix, oth_mix, hyena_out, parts)
    got_half = swap(give_half, "dp", 1)
    gain = attn_gain[None]
    total, power, own_rows = qkv_half(where, own_half, own_hot, base, gain, qkv_proj)
    *heads, oth_rows = qkv_half(
        where, got_half, own_hot, base, gain, qkv_proj, (total, power, cosine, sine)
    )

    pieces = [heads[0]] + [swap(heads[rel], "context", rel) for rel in range(1, 4)]
    attended = attend(place, pieces)
    mine = jnp.concatenate(
        [attended[0]]
        + [swap(attended[rel], "context", rel) for rel in range(1, 4)],
        axis=1,
    ).reshape(4, 128, 512)

    def rows_for(rel):
        return lax.dynamic_index_in_dim(mine, plane ^ rel, 0, keepdims=False)

    own_att = jnp.concatenate(
        [rows_for(0)] + [swap(rows_for(rel), "tensor", rel) for rel in range(1, 4)],
        axis=1,
    )
    oth_att = swap(own_att, "dp", 1)

    cross = (ctx & 1) ^ (ctx >> 1)
    late_lane, _ = lax.optimization_barrier((half_lane + cross * 1024, coef))
    units = along_chain(rows_of(attn_out, late_lane, 1024), edge)
    parts = []
    for unit in units:
        parts += [unit, swap(unit[:, :512], "context", 1), swap(unit[:, 512:], "context", 2)]
    own_out, give_out = out_branches(where, own_att, oth_att, own_rows, attn_out, parts)
    got_out = swap(give_out, "dp", 1)
    return join_halves(where, own_out, oth_rows, got_out)


def solution(mesh):
    grid_shape = dict(mesh.shape)
    square = (grid_shape["dp"], grid_shape["context"], grid_shape["tensor"]) == (2, 4, 4)
    body = block_body if square else generic_body
    placed = (
        P(("dp", "context", "tensor")),
        P("dp"),
        P(),
        P(),
        P(None, None, "tensor"),
        P(None, None, "tensor"),
        P("tensor", None),
        P("tensor"),
        P("tensor", None),
        P(),
        P(None, None, "tensor"),
        P("tensor", None),
    )
    return jax.shard_map(
        body,
        mesh=mesh,
        in_specs=placed,
        out_specs=P(("dp", "context", "tensor"), None),
        check_vma=False,
    )
```

```python
import functools
import math

import jax
import jax.numpy as jnp
import numpy as np
from jax import lax
from jax.experimental import pallas as pl
from jax.experimental.pallas import tpu as pltpu
from jax.sharding import PartitionSpec as P

HD = 128
GROUP_CH = 16


EPS = 1e-06
THETA = 1000000.0
NEG_FILL = -1e30


def rms_scale(row_data, gain_vec):
    values = row_data.astype(jnp.float32)
    factor = lax.rsqrt(jnp.mean(values * values, axis=-1, keepdims=True) + EPS)
    return (values * factor * gain_vec).astype(jnp.bfloat16)


def toeplitz(long_filter):
    filter_len = long_filter.shape[1]
    tap_lag = (
        jnp.arange(filter_len, dtype=jnp.int32)[:, None]
        - jnp.arange(filter_len, dtype=jnp.int32)[None, :]
    )
    near_taps = jnp.take(long_filter, jnp.clip(tap_lag, 0, filter_len - 1), axis=1)
    far_taps = jnp.take(long_filter, jnp.clip(tap_lag + filter_len, 0, filter_len - 1), axis=1)
    near_taps = jnp.where(tap_lag[None] >= 0, near_taps, jnp.zeros_like(near_taps))
    far_taps = jnp.where(tap_lag[None] < 0, far_taps, jnp.zeros_like(far_taps))
    return (near_taps, far_taps)


def long_conv(padded, long_filter, group_width):
    filter_len = long_filter.shape[1]
    near_taps, far_taps = toeplitz(long_filter)
    row_total = padded.shape[0]
    chan_total = padded.shape[1]
    blocks = padded.reshape(
        row_total // filter_len, filter_len, chan_total // group_width, group_width
    )
    current_part = jnp.einsum(
        "grs,bsgc->brgc", near_taps, blocks[1:], precision=lax.Precision.HIGHEST
    )
    before = jnp.einsum("grs,bsgc->brgc", far_taps, blocks[:-1], precision=lax.Precision.HIGHEST)
    return (current_part + before).reshape(row_total - filter_len, chan_total)


def short_conv(padded_rows, short_filter, out_len):
    taps = short_filter.shape[1]
    result = jnp.zeros((padded_rows.shape[0], out_len, padded_rows.shape[2]), jnp.float32)
    for tap_at in range(taps):
        offset = taps - 1 - tap_at
        result = (
            result + short_filter[:, tap_at][:, None, :] * padded_rows[:, offset : offset + out_len]
        )
    return result


def rotate(values, positions, head_dim):
    half_dim = head_dim // 2
    inverse_freq = THETA ** (-(2.0 * jnp.arange(half_dim, dtype=jnp.float32)) / head_dim)
    angles = positions.astype(jnp.float32)[:, None] * inverse_freq[None, :]
    cosine_part = jnp.cos(angles)[:, None, :]
    sine_part = jnp.sin(angles)[:, None, :]
    lower_half = values[..., :half_dim]
    upper_half = values[..., half_dim:]
    return jnp.concatenate(
        [
            lower_half * cosine_part - upper_half * sine_part,
            upper_half * cosine_part + lower_half * sine_part,
        ],
        axis=-1,
    )


def generic_body(
    ids,
    block_order,
    embed,
    mix_gain,
    in_proj,
    short_filter,
    long_filter,
    conv_skip,
    hyena_out,
    attn_gain,
    qkv_proj,
    attn_out,
):
    tok_rows = ids.shape[0]
    tensor_count = lax.axis_size("tensor")
    context_count = lax.axis_size("context")
    ctx_rows = tok_rows * tensor_count
    block_rows = ctx_rows // 2
    filter_len = long_filter.shape[1]
    short_len = short_filter.shape[1]
    halo_len = filter_len + short_len - 2
    chan_local = in_proj.shape[2]
    context_at = lax.axis_index("context")
    vocab_ids = jnp.arange(embed.shape[0], dtype=jnp.int32)
    chosen = (ids[:, None] == vocab_ids[None, :]).astype(jnp.bfloat16)
    embedded = jnp.dot(chosen, embed, preferred_element_type=jnp.float32).astype(jnp.bfloat16)
    embedded_all = lax.all_gather(embedded, "tensor", axis=0, tiled=True)
    mixed_in = rms_scale(embedded_all, mix_gain)
    projected = jnp.einsum(
        "rd,jdc->jrc", mixed_in, in_proj, preferred_element_type=jnp.float32
    ).astype(jnp.bfloat16)
    slot_ids = jnp.arange(2 * context_count, dtype=jnp.int32)
    slot_pair = 2 * context_at + jnp.arange(2, dtype=jnp.int32)
    owned_blocks = jnp.sum(
        jnp.where(slot_ids[None, :] == slot_pair[:, None], block_order[None, :], 0), axis=1
    )
    local_pos = (
        owned_blocks[:, None] * block_rows + jnp.arange(block_rows, dtype=jnp.int32)[None, :]
    ).reshape(ctx_rows)
    tail_rows = jnp.stack(
        [projected[:, block_rows - halo_len : block_rows], projected[:, ctx_rows - halo_len :]]
    )
    all_tails = lax.all_gather(tail_rows, "context", axis=0, tiled=True)
    out_len = filter_len - 1 + block_rows
    pieces = []
    for block_at in range(2):
        holder_hit = (block_order == owned_blocks[block_at] - 1).astype(jnp.bfloat16)
        before_rows = jnp.einsum(
            "s,sjrc->jrc", holder_hit, all_tails, preferred_element_type=jnp.float32
        )
        own_rows = projected[:, block_at * block_rows : (block_at + 1) * block_rows].astype(
            jnp.float32
        )
        extended = jnp.concatenate([before_rows, own_rows], axis=1)
        filtered = short_conv(extended, short_filter, out_len)
        gated_rows = filtered[1] * filtered[2]
        padded = jnp.concatenate([jnp.zeros((1, chan_local), jnp.float32), gated_rows], axis=0)
        long_mix = long_conv(padded, long_filter, GROUP_CH)
        own_gate = gated_rows[filter_len - 1 :]
        pieces.append(
            (filtered[0, filter_len - 1 :] * (long_mix + conv_skip * own_gate)).astype(jnp.bfloat16)
        )
    hyena_mix = jnp.concatenate(pieces, axis=0)
    hyena_own = lax.psum_scatter(
        jnp.dot(hyena_mix, hyena_out, preferred_element_type=jnp.float32),
        "tensor",
        scatter_dimension=0,
        tiled=True,
    )
    stream_own = embedded.astype(jnp.float32) + hyena_own
    stream_all = lax.all_gather(stream_own, "tensor", axis=0, tiled=True)
    attn_in = rms_scale(stream_all, attn_gain)
    projections = jnp.einsum("rd,jdf->jrf", attn_in, qkv_proj, preferred_element_type=jnp.float32)
    local_heads = projections.shape[2] // HD
    shaped = projections.reshape(3, ctx_rows, local_heads, HD)
    queries = rotate(shaped[0], local_pos, HD).astype(jnp.bfloat16)
    keys_flat = (
        rotate(shaped[1], local_pos, HD).astype(jnp.bfloat16).reshape(ctx_rows, local_heads * HD)
    )
    values_flat = shaped[2].astype(jnp.bfloat16).reshape(ctx_rows, local_heads * HD)
    score_scale = HD ** (-0.5)
    start_state = (
        jnp.full((2, block_rows, local_heads), NEG_FILL, jnp.float32),
        jnp.zeros((2, block_rows, local_heads), jnp.float32),
        jnp.zeros((2, block_rows, local_heads, HD), jnp.float32),
    )
    key_piece = lax.all_gather(keys_flat, "context", axis=0, tiled=True)
    value_piece = lax.all_gather(values_flat, "context", axis=0, tiled=True)
    piece_len = key_piece.shape[0]
    sub_len = math.gcd(piece_len, 512)

    def attend_sub(sub_index, carried):
        key_block = lax.dynamic_slice_in_dim(key_piece, sub_index * sub_len, sub_len, 0).reshape(
            sub_len, local_heads, HD
        )
        value_block = lax.dynamic_slice_in_dim(
            value_piece, sub_index * sub_len, sub_len, 0
        ).reshape(sub_len, local_heads, HD)
        row_ids = sub_index * sub_len + jnp.arange(sub_len, dtype=jnp.int32)
        holder = row_ids // block_rows
        key_pos = (
            jnp.sum(
                jnp.where(holder[:, None] == slot_ids[None, :], block_order[None, :], 0), axis=1
            )
            * block_rows
            + row_ids % block_rows
        )
        top_all, sums_all, weighted_all = carried
        outputs = []
        for block_at in range(2):
            query_rows = queries[block_at * block_rows : (block_at + 1) * block_rows]
            query_pos = local_pos[block_at * block_rows : (block_at + 1) * block_rows]
            top_score = top_all[block_at]
            weight_sum = sums_all[block_at]
            weighted = weighted_all[block_at]
            scores = (
                jnp.einsum(
                    "qhd,khd->qhk", query_rows, key_block, preferred_element_type=jnp.float32
                )
                * score_scale
            )
            visible = key_pos[None, None, :] <= query_pos[:, None, None]
            scores = jnp.where(visible, scores, NEG_FILL)
            new_top = jnp.maximum(top_score, jnp.max(scores, axis=-1))
            rescale = jnp.exp(top_score - new_top)
            weights = jnp.where(visible, jnp.exp(scores - new_top[..., None]), 0.0)
            weight_sum = weight_sum * rescale + jnp.sum(weights, axis=-1)
            weighted = weighted * rescale[..., None] + jnp.einsum(
                "qhk,khd->qhd",
                weights.astype(jnp.bfloat16),
                value_block,
                preferred_element_type=jnp.float32,
            )
            result = (new_top, weight_sum, weighted)
            outputs.append(result)
        return tuple((jnp.stack([entry[field] for entry in outputs]) for field in range(3)))

    _, sums_final, weighted_final = lax.fori_loop(0, piece_len // sub_len, attend_sub, start_state)
    attended = (
        (weighted_final / sums_final[..., None])
        .astype(jnp.bfloat16)
        .reshape(ctx_rows, local_heads * HD)
    )
    attn_own = lax.psum_scatter(
        jnp.dot(attended, attn_out, preferred_element_type=jnp.float32).astype(jnp.bfloat16),
        "tensor",
        scatter_dimension=0,
        tiled=True,
    ).astype(jnp.float32)
    return stream_own + attn_own


CODES = (65, 67, 71, 84)
BF16 = jnp.bfloat16
F32 = jnp.float32
VM = pl.BlockSpec(memory_space=pltpu.VMEM)
SM = pl.BlockSpec(memory_space=pltpu.SMEM)

UNIT, CTX, PLANE, CROSS, HALF = 0, 4, 8, 12, 13
MINE, THEIRS, SLOTS = 15, 17, 19


def position_table():
    rows = []
    for half in range(2):
        for ctx in range(4):
            for plane in range(4):
                units = [plane, (1, 0, 3, 2)[plane], (2, 2, 1, 1)[plane], (3, 3, 0, 0)[plane]]
                row = units + [ctx ^ rel for rel in range(4)] + [plane ^ rel for rel in range(4)]
                row += [(ctx & 1) ^ (ctx >> 1), half, 1 - half]
                row += [2 * half, 2 * half + 1, 2 - 2 * half, 3 - 2 * half]
                row += [2 * (ctx ^ rel) + at for rel in range(4) for at in range(2)]
                rows.append(row)
    return np.array(rows, np.int32)


def swap(value, axis, mask):
    size = lax.axis_size(axis)
    return lax.ppermute(value, axis, [(at, at ^ mask) for at in range(size)])


def rows_of(weights, lane_start, width):
    return lax.dynamic_slice(weights, (0, lane_start), (weights.shape[0], width))


def along_chain(piece, edge_plane):
    middle = [(1, 2), (2, 1)]
    outward = [(1, 0), (2, 3)]
    near = swap(piece, "tensor", 1)
    across = lax.ppermute(piece, "tensor", middle)
    far_mid = lax.ppermute(near, "tensor", middle)
    across_out = lax.ppermute(across, "tensor", outward)
    far_out = lax.ppermute(far_mid, "tensor", outward)
    return (
        near,
        jnp.where(edge_plane, across_out, across),
        jnp.where(edge_plane, far_out, far_mid),
    )


def dot32(left, right):
    return jnp.dot(left, right, preferred_element_type=F32)


def hyena_kernel(where_ref, coef_ref, hot_ref, taps_ref, skip_ref, mix_ref):
    hot = hot_ref[...]
    first, second, third = (dot32(coef_ref[j], hot) for j in range(3))
    gated = second * third
    packed = gated.astype(BF16)
    row = lax.broadcasted_iota(jnp.int32, (128, 128), 0)
    lane = lax.broadcasted_iota(jnp.int32, (128, 128), 1)
    near = lane >= row
    mixed = []
    for group in range(16):
        spread = jnp.broadcast_to(taps_ref[group : group + 1, :], (128, 128))
        rolled = pltpu.roll(spread, 0, 1, stride=1, stride_axis=0)
        zero = jnp.zeros_like(rolled)
        matrix = jnp.concatenate(
            [jnp.where(near, zero, rolled), jnp.where(near, rolled, zero)], axis=0
        ).astype(BF16)
        chans = packed[16 * group : 16 * group + 16]
        left = jnp.concatenate(
            [chans[:, at : at + 256] for at in (0, 128, 384, 512)], axis=0
        )
        result = dot32(left, matrix)
        mixed.append(jnp.concatenate([result[16 * i : 16 * i + 16] for i in range(4)], axis=1))
    long_mix = jnp.concatenate(mixed, axis=0)
    own_gate = jnp.concatenate([gated[:, 128:384], gated[:, 512:768]], axis=1)
    own_first = jnp.concatenate([first[:, 128:384], first[:, 512:768]], axis=1)
    mix = own_first * (long_mix + skip_ref[...] * own_gate)
    mix_ref[...] = mix.T.astype(BF16)


def hyena_mixes(where, coef, hot, taps, skip):
    chans = coef.shape[1]
    step = 256
    return pl.pallas_call(
        hyena_kernel,
        grid_spec=pltpu.PrefetchScalarGridSpec(
            num_scalar_prefetch=1,
            grid=(chans // step,),
            in_specs=[
                pl.BlockSpec((3, step, coef.shape[2]), lambda i, w: (0, i, 0)),
                pl.BlockSpec(hot.shape, lambda i, w: (0, 0)),
                pl.BlockSpec((step // 16, 128), lambda i, w: (i, 0)),
                pl.BlockSpec((step, 1), lambda i, w: (i, 0)),
            ],
            out_specs=pl.BlockSpec(
                (512, step), lambda i, w: (0, w[PLANE + i // 2] * 2 + i % 2)
            ),
        ),
        out_shape=jax.ShapeDtypeStruct((512, chans), BF16),
        name="hyena_mix",
    )(where, coef, hot, taps, skip)


def both(own_ref, oth_ref):
    return jnp.concatenate([own_ref[...], oth_ref[...]], axis=0)


def branch_lane(where_ref, rel):
    return pl.ds(pl.multiple_of(where_ref[CTX + rel] * 512, 512), 512)


def branch_a_kernel(where_ref, own0, oth0, own1, oth1, own2, oth2, home_ref, *refs):
    block1, block2, sum_ref = refs[:5], refs[5:9], refs[9]
    left0, left1, left2 = both(own0, oth0), both(own1, oth1), both(own2, oth2)
    rows = own0.shape[0]
    for rel in range(4):
        lane = branch_lane(where_ref, rel)
        total = dot32(left0, home_ref[:, lane])
        if rel < 3:
            total += dot32(left1, block1[rel][...])
        else:
            total += dot32(left1[:, :256], block1[3][...])
            total += dot32(left1[:, 256:], block1[4][...])
        total += dot32(left2, block2[rel][...])
        sum_ref[0, :, lane] = total[:rows]
        sum_ref[1, :, lane] = total[rows:]


def branch_b_kernel(where_ref, own3, oth3, sum_ref, *refs):
    block3, (own_ref, oth_ref) = refs[:4], refs[4:]
    left3 = both(own3, oth3)
    rows = own3.shape[0]
    for rel in range(4):
        lane = branch_lane(where_ref, rel)
        total = dot32(left3, block3[rel][...])
        own_ref[:, lane] = sum_ref[0, :, lane] + total[:rows]
        oth_ref[:, lane] = (sum_ref[1, :, lane] + total[rows:]).astype(BF16)


def hyena_branches(where, own_mix, oth_mix, home, parts):
    tile = 256
    grid = (512 // tile,)

    def mixes(at):
        return [pl.BlockSpec((tile, 512), lambda i, w: (i, w[UNIT + at]))] * 2

    sums = pl.BlockSpec((2, tile, 2048), lambda i, w: (0, i, 0))
    flat = pl.BlockSpec((tile, 2048), lambda i, w: (i, 0))
    sum_shape = jax.ShapeDtypeStruct((2, 512, 2048), F32)
    half_shapes = [
        jax.ShapeDtypeStruct((512, 2048), F32),
        jax.ShapeDtypeStruct((512, 2048), BF16),
    ]

    def call(kernel, in_specs, out_specs, out_shape, operands):
        return pl.pallas_call(
            kernel,
            grid_spec=pltpu.PrefetchScalarGridSpec(
                num_scalar_prefetch=1, grid=grid, in_specs=in_specs, out_specs=out_specs
            ),
            out_shape=out_shape,
            name="hyena_branch",
        )(where, *operands)

    mix = [own_mix, oth_mix]
    home_spec = pl.BlockSpec((512, 2048), lambda i, w: (0, w[HALF]))
    partial = call(
        branch_a_kernel,
        mixes(0) + mixes(1) + mixes(2) + [home_spec] + [VM] * 9,
        sums,
        sum_shape,
        mix * 3 + [home] + parts[0] + parts[1],
    )
    return call(
        branch_b_kernel,
        mixes(3) + [sums] + [VM] * 4,
        [flat, flat],
        half_shapes,
        mix + [partial] + parts[2],
    )


def qkv_kernel(where_ref, half_ref, hot_ref, base_ref, gain_ref, proj_ref, *refs, first):
    at = pl.program_id(0)
    if first:
        total_ref, power_ref, rows_ref, block_ref = refs
    else:
        part_ref, part_power_ref, cos_ref, sin_ref = refs[:4]
        head_refs = refs[4:8]
        rows_ref, total_ref, power_ref, block_ref = refs[8:]

    @pl.when(at == 0)
    def _():
        if first:
            total_ref[...] = jnp.zeros_like(total_ref)
            power_ref[...] = jnp.zeros_like(power_ref)
        else:
            total_ref[...] = part_ref[...]
            power_ref[...] = part_power_ref[...]

    stream = dot32(hot_ref[...], base_ref[...]) + half_ref[...].astype(F32)
    block_ref[...] = stream
    rows_ref[...] = block_ref[pl.ds(pl.multiple_of(where_ref[PLANE] * 128, 128), 128), :]
    power_ref[...] += jnp.sum(stream * stream, axis=1, keepdims=True)
    scaled = (stream * gain_ref[...]).astype(BF16)
    for j in range(3):
        total_ref[:, 512 * j : 512 * j + 512] += dot32(scaled, proj_ref[j])
    if first:
        return

    @pl.when(at == 1)
    def _():
        factor = lax.rsqrt(power_ref[...] * (1.0 / 4096.0) + EPS)
        cosine = cos_ref[...] * factor
        sine = sin_ref[...] * factor
        for rel in range(4):
            for j in range(3):
                lane = pl.multiple_of(where_ref[CTX + rel] * 128 + 512 * j, 128)
                piece = total_ref[:, pl.ds(lane, 128)]
                if j < 2:
                    piece = piece * cosine + pltpu.roll(piece, 64, 1) * sine
                else:
                    piece = piece * factor
                head_refs[rel][:, 128 * j : 128 * j + 128] = piece.astype(BF16)


def qkv_half(where, half, hot, base, gain, proj, extra=()):
    first = not extra
    at = MINE if first else THEIRS
    whole = lambda shape: pl.BlockSpec(shape, lambda i, w: (0,) * len(shape))
    in_specs = [
        pl.BlockSpec((512, 1024), lambda i, w: (0, i)),
        whole(hot.shape),
        pl.BlockSpec((base.shape[0], 1024), lambda i, w: (0, w[at + i])),
        pl.BlockSpec((1, 1024), lambda i, w: (0, w[at + i])),
        pl.BlockSpec((3, 1024, 512), lambda i, w: (0, w[at + i], 0)),
    ]
    rows_spec = pl.BlockSpec((128, 1024), lambda i, w: (0, i))
    rows_shape = jax.ShapeDtypeStruct((128, 2048), F32)
    scratch = [pltpu.VMEM((512, 1024), F32)]
    if first:
        out_specs = [whole((512, 1536)), whole((512, 1)), rows_spec]
        out_shape = [
            jax.ShapeDtypeStruct((512, 1536), F32),
            jax.ShapeDtypeStruct((512, 1), F32),
            rows_shape,
        ]
    else:
        in_specs += [whole(value.shape) for value in extra]
        out_specs = [whole((512, 384))] * 4 + [rows_spec]
        out_shape = [jax.ShapeDtypeStruct((512, 384), BF16)] * 4 + [rows_shape]
        scratch = [pltpu.VMEM((512, 1536), F32), pltpu.VMEM((512, 1), F32)] + scratch
    return pl.pallas_call(
        functools.partial(qkv_kernel, first=first),
        grid_spec=pltpu.PrefetchScalarGridSpec(
            num_scalar_prefetch=1,
            grid=(2,),
            in_specs=in_specs,
            out_specs=out_specs,
            scratch_shapes=scratch,
        ),
        out_shape=out_shape,
        name="qkv_half",
    )(where, half, hot, base, gain, proj, *extra)


def attend_kernel(slot_ref, *refs):
    x_refs, out_refs, (q_ref, k_ref, v_ref, mixed_ref) = refs[:4], refs[4:8], refs[8:]
    for rel, x_ref in enumerate(x_refs):
        for half in range(2):
            base = pl.multiple_of(slot_ref[2 * rel + half] * 256, 256)
            rows = slice(256 * half, 256 * half + 256)
            q_ref[pl.ds(base, 256), :] = x_ref[rows, 0:128]
            k_ref[pl.ds(base, 256), :] = x_ref[rows, 128:256]
            v_ref[pl.ds(base, 256), :] = x_ref[rows, 256:384]
    row = lax.broadcasted_iota(jnp.int32, (256, 256), 0)
    lane = lax.broadcasted_iota(jnp.int32, (256, 256), 1)
    causal = lane <= row
    scale = HD ** (-0.5)
    for block in range(8):
        width = 256 * block + 256
        query = q_ref[256 * block : width, :]
        scores = lax.dot_general(
            query, k_ref[0:width, :], (((1,), (1,)), ((), ())), preferred_element_type=F32
        )
        last = jnp.where(causal, scores[:, width - 256 :], NEG_FILL)
        if block > 0:
            scores = jnp.concatenate([scores[:, : width - 256], last], axis=1)
        else:
            scores = last
        top = jnp.max(scores, axis=1, keepdims=True)
        weights = jnp.exp((scores - top) * scale)
        total = jnp.sum(weights, axis=1, keepdims=True)
        mixed = dot32(weights.astype(BF16), v_ref[0:width, :])
        mixed_ref[256 * block : width, :] = (mixed / total).astype(BF16)
    for rel, out_ref in enumerate(out_refs):
        for half in range(2):
            base = pl.multiple_of(slot_ref[2 * rel + half] * 256, 256)
            out_ref[256 * half : 256 * half + 256, :] = mixed_ref[pl.ds(base, 256), :]


def attend(slots, pieces):
    return pl.pallas_call(
        attend_kernel,
        in_specs=[SM] + [VM] * 4,
        out_specs=[VM] * 4,
        out_shape=[jax.ShapeDtypeStruct((512, 128), BF16)] * 4,
        scratch_shapes=[pltpu.VMEM((2048, 128), BF16)] * 4,
        name="attend",
    )(slots, *pieces)


def out_kernel(where_ref, own_ref, oth_ref, rows_ref, home_ref, *refs):
    parts, refs = refs[:9], refs[9:]
    own_out_ref, oth_out_ref, left_ref, home_vm, *rest = refs
    held, sem = rest[:9], rest[9]
    lane = pl.multiple_of(where_ref[HALF] * 2048, 2048)
    copies = [pltpu.make_async_copy(home_ref.at[:, pl.ds(lane, 2048)], home_vm, sem.at[9])]
    copies += [
        pltpu.make_async_copy(part, room, sem.at[at])
        for at, (part, room) in enumerate(zip(parts, held))
    ]
    copies[0].start()
    for kind in range(3):
        for unit in range(3):
            copies[1 + 3 * unit + kind].start()
    for side, src_ref in enumerate((own_ref, oth_ref)):
        for far in range(4):
            for rel in range(4):
                head = where_ref[PLANE + far] * 4 + where_ref[CTX + rel]
                lane = pl.multiple_of(head * 128, 128)
                at = 512 * far + 128 * rel
                left_ref[128 * side : 128 * side + 128, pl.ds(lane, 128)] = src_ref[
                    :, at : at + 128
                ]

    def left(unit):
        return left_ref[:, pl.ds(pl.multiple_of(where_ref[UNIT + unit] * 512, 512), 512)]

    lanes = []
    copies[0].wait()
    for quarter in range(4):
        half = where_ref[CROSS] if quarter < 2 else 1 - where_ref[CROSS]
        lanes.append(pl.multiple_of(half * 1024 + (quarter % 2) * 512, 512))
        own_out_ref[:, pl.ds(lanes[quarter], 512)] = rows_ref[:, pl.ds(lanes[quarter], 512)]
    for quarter in range(4):
        for unit in range(3):
            if quarter != 1:
                copies[1 + 3 * unit + max(quarter - 1, 0)].wait()
        total = dot32(left(0), home_vm[:, pl.ds(lanes[quarter], 512)])
        for unit in range(3):
            block, side_x, side_y = held[3 * unit : 3 * unit + 3]
            if quarter < 2:
                right = block[:, 512 * quarter : 512 * quarter + 512]
            else:
                right = (side_x, side_y)[quarter - 2][...]
            total += dot32(left(unit + 1), right)
        own_out_ref[:, pl.ds(lanes[quarter], 512)] += total[:128]
        oth_out_ref[:, pl.ds(lanes[quarter], 512)] = total[128:].astype(oth_out_ref.dtype)


def out_branches(where, own, oth, rows, home, parts):
    anywhere = pl.BlockSpec(memory_space=pl.ANY)
    flat = pl.BlockSpec((128, 2048), lambda i, w: (0, 0))
    return pl.pallas_call(
        out_kernel,
        grid_spec=pltpu.PrefetchScalarGridSpec(
            num_scalar_prefetch=1,
            grid=(1,),
            in_specs=[flat, flat, flat] + [anywhere] * (1 + len(parts)),
            out_specs=[pl.BlockSpec((128, 2048), lambda i, w: (0, w[HALF])), flat],
            scratch_shapes=[pltpu.VMEM((256, 2048), BF16), pltpu.VMEM((512, 2048), BF16)]
            + [pltpu.VMEM(part.shape, BF16) for part in parts]
            + [pltpu.SemaphoreType.DMA((10,))],
        ),
        out_shape=[jax.ShapeDtypeStruct((128, 4096), F32), jax.ShapeDtypeStruct((128, 2048), BF16)],
        name="out_branch",
    )(where, own, oth, rows, home, *parts)


def block_body(*operands):
    return block_rows_out(*operands)


def block_rows_out(
    ids,
    block_order,
    embed,
    mix_gain,
    in_proj,
    short_filter,
    long_filter,
    conv_skip,
    hyena_out,
    attn_gain,
    qkv_proj,
    attn_out,
):
    half_at = lax.axis_index("dp")
    ctx = lax.axis_index("context")
    plane = lax.axis_index("tensor")
    edge = jnp.logical_or(plane == 0, plane == 3)
    order = block_order.astype(jnp.int32)
    half_lane = half_at * 2048
    table_rows = jnp.asarray(position_table())
    where = lax.dynamic_index_in_dim(table_rows, half_at * 16 + ctx * 4 + plane, 0, keepdims=False)

    piece = rows_of(hyena_out, half_lane + ctx * 512, 512)
    parts = []
    for at, unit in enumerate(along_chain(piece, edge)):
        side_x = swap(unit, "context", 1)
        side_y = swap(unit, "context", 2)
        if at == 0:
            corner = [swap(side_y[:256], "context", 1), swap(side_x[256:], "context", 2)]
        else:
            corner = [swap(unit, "context", 3)]
        parts.append([unit, side_x, side_y] + corner)

    own_row = ids.astype(F32).reshape(1, 128)
    id_rows = jnp.concatenate(
        [own_row] + [swap(own_row, "context", rel) for rel in range(1, 4)], axis=1
    )

    base = jnp.concatenate([embed[code : code + 1] for code in CODES], axis=0)
    mixed_in = rms_scale(base, mix_gain)
    table = jnp.einsum(
        "rd,jdc->jrc", mixed_in, in_proj, preferred_element_type=F32
    ).astype(BF16)
    packed = jnp.concatenate(
        [
            table.astype(F32).reshape(12, 512),
            short_filter.reshape(9, 512),
            conv_skip.reshape(1, 512),
            long_filter.reshape(8, 512),
            id_rows,
        ],
        axis=0,
    )
    everything = jnp.stack([packed] + [swap(packed, "tensor", rel) for rel in range(1, 4)])
    slot_ids = jnp.arange(8, dtype=jnp.int32)
    place = jnp.sum(
        jnp.where(where[SLOTS : SLOTS + 8, None] == slot_ids[None, :], order[None, :], 0), axis=1
    )
    owned = place[:2]
    local_pos = (
        owned[:, None] * 256 + jnp.arange(256, dtype=jnp.int32)[None, :]
    ).reshape(512)
    inverse_freq = THETA ** (-(2.0 * jnp.arange(64, dtype=F32)) / HD)
    angles = local_pos.astype(F32)[:, None] * inverse_freq[None, :]
    cosine = jnp.cos(angles)
    sine = jnp.sin(angles)
    cosine = jnp.concatenate([cosine, cosine], axis=1)
    sine = jnp.concatenate([-sine, sine], axis=1)
    which = where[None, PLANE : PLANE + 4] == jnp.arange(4, dtype=jnp.int32)[:, None]
    plane_ids = everything[:, 30].reshape(1, 4, 4, 128)
    plane_ids = jnp.sum(jnp.where(which[:, :, None, None], plane_ids, 0.0), axis=1)
    all_ids = plane_ids.transpose(1, 0, 2).reshape(8, 256)
    tables = everything[:, :12].reshape(4, 3, 1, 4, 512)
    shorts = everything[:, 12:21].reshape(4, 3, 3, 1, 512)
    coef = (tables * shorts).transpose(1, 0, 4, 2, 3).reshape(3, 2048, 12)
    coarse = lax.reduce_precision(coef, 8, 7)
    coef = jnp.concatenate([coarse, coef - coarse], axis=2).astype(BF16)
    skip = everything[:, 21].reshape(2048, 1)
    taps = everything[:, 22:30].reshape(128, 128)

    before_hit = place[None, :] == owned[:, None] - 1
    own_ids = all_ids[:2]
    before_ids = jnp.sum(jnp.where(before_hit[:, :, None], all_ids[None], 0.0), axis=1)
    span = jnp.concatenate([before_ids, own_ids], axis=1)
    codes = jnp.array(CODES, F32)
    hot = jnp.stack(
        [
            (span[None, :, 128 - lag : 512 - lag] == codes[:, None, None]).astype(BF16)
            for lag in range(3)
        ]
    ).reshape(12, 768)
    hot = jnp.concatenate([hot, hot], axis=0)
    own_hot = (own_ids.reshape(512, 1) == codes[None, :]).astype(BF16)
    coef, hot, place, cosine, sine, own_hot, base = lax.optimization_barrier(
        (coef, hot, place, cosine, sine, own_hot, base)
    )

    own_mix = hyena_mixes(where, coef, hot, taps, skip)
    oth_mix = swap(own_mix, "dp", 1)

    own_half, give_half = hyena_branches(where, own_mix, oth_mix, hyena_out, parts)
    got_half = swap(give_half, "dp", 1)
    gain = attn_gain[None]
    total, power, own_rows = qkv_half(where, own_half, own_hot, base, gain, qkv_proj)
    *heads, oth_rows = qkv_half(
        where, got_half, own_hot, base, gain, qkv_proj, (total, power, cosine, sine)
    )

    pieces = [heads[0]] + [swap(heads[rel], "context", rel) for rel in range(1, 4)]
    attended = attend(place, pieces)
    mine = jnp.concatenate(
        [attended[0]]
        + [swap(attended[rel], "context", rel) for rel in range(1, 4)],
        axis=1,
    ).reshape(4, 128, 512)

    def rows_for(rel):
        return lax.dynamic_index_in_dim(mine, plane ^ rel, 0, keepdims=False)

    own_att = jnp.concatenate(
        [rows_for(0)] + [swap(rows_for(rel), "tensor", rel) for rel in range(1, 4)],
        axis=1,
    )
    oth_att = swap(own_att, "dp", 1)

    cross = (ctx & 1) ^ (ctx >> 1)
    late_lane, _ = lax.optimization_barrier((half_lane + cross * 1024, coef))
    units = along_chain(rows_of(attn_out, late_lane, 1024), edge)
    parts = []
    for unit in units:
        parts += [unit, swap(unit[:, :512], "context", 1), swap(unit[:, 512:], "context", 2)]
    own_out, give_out = out_branches(where, own_att, oth_att, own_rows, attn_out, parts)
    got_out = swap(give_out, "dp", 1)
    return lax.dynamic_update_slice(
        own_out, oth_rows + got_out.astype(F32), (0, (1 - half_at) * 2048)
    )


def solution(mesh):
    grid_shape = dict(mesh.shape)
    square = (grid_shape["dp"], grid_shape["context"], grid_shape["tensor"]) == (2, 4, 4)
    body = block_body if square else generic_body
    placed = (
        P(("dp", "context", "tensor")),
        P("dp"),
        P(),
        P(),
        P(None, None, "tensor"),
        P(None, None, "tensor"),
        P("tensor", None),
        P("tensor"),
        P("tensor", None),
        P(),
        P(None, None, "tensor"),
        P("tensor", None),
    )
    return jax.shard_map(
        body,
        mesh=mesh,
        in_specs=placed,
        out_specs=P(("dp", "context", "tensor"), None),
        check_vma=False,
    )
```

```python
import functools
import math

import jax
import jax.numpy as jnp
import numpy as np
from jax import lax
from jax.experimental import pallas as pl
from jax.experimental.pallas import tpu as pltpu
from jax.sharding import PartitionSpec as P

HD = 128
GROUP_CH = 16


EPS = 1e-06
THETA = 1000000.0
NEG_FILL = -1e30


def rms_scale(row_data, gain_vec):
    values = row_data.astype(jnp.float32)
    factor = lax.rsqrt(jnp.mean(values * values, axis=-1, keepdims=True) + EPS)
    return (values * factor * gain_vec).astype(jnp.bfloat16)


def toeplitz(long_filter):
    filter_len = long_filter.shape[1]
    tap_lag = (
        jnp.arange(filter_len, dtype=jnp.int32)[:, None]
        - jnp.arange(filter_len, dtype=jnp.int32)[None, :]
    )
    near_taps = jnp.take(long_filter, jnp.clip(tap_lag, 0, filter_len - 1), axis=1)
    far_taps = jnp.take(long_filter, jnp.clip(tap_lag + filter_len, 0, filter_len - 1), axis=1)
    near_taps = jnp.where(tap_lag[None] >= 0, near_taps, jnp.zeros_like(near_taps))
    far_taps = jnp.where(tap_lag[None] < 0, far_taps, jnp.zeros_like(far_taps))
    return (near_taps, far_taps)


def long_conv(padded, long_filter, group_width):
    filter_len = long_filter.shape[1]
    near_taps, far_taps = toeplitz(long_filter)
    row_total = padded.shape[0]
    chan_total = padded.shape[1]
    blocks = padded.reshape(
        row_total // filter_len, filter_len, chan_total // group_width, group_width
    )
    current_part = jnp.einsum(
        "grs,bsgc->brgc", near_taps, blocks[1:], precision=lax.Precision.HIGHEST
    )
    before = jnp.einsum("grs,bsgc->brgc", far_taps, blocks[:-1], precision=lax.Precision.HIGHEST)
    return (current_part + before).reshape(row_total - filter_len, chan_total)


def short_conv(padded_rows, short_filter, out_len):
    taps = short_filter.shape[1]
    result = jnp.zeros((padded_rows.shape[0], out_len, padded_rows.shape[2]), jnp.float32)
    for tap_at in range(taps):
        offset = taps - 1 - tap_at
        result = (
            result + short_filter[:, tap_at][:, None, :] * padded_rows[:, offset : offset + out_len]
        )
    return result


def rotate(values, positions, head_dim):
    half_dim = head_dim // 2
    inverse_freq = THETA ** (-(2.0 * jnp.arange(half_dim, dtype=jnp.float32)) / head_dim)
    angles = positions.astype(jnp.float32)[:, None] * inverse_freq[None, :]
    cosine_part = jnp.cos(angles)[:, None, :]
    sine_part = jnp.sin(angles)[:, None, :]
    lower_half = values[..., :half_dim]
    upper_half = values[..., half_dim:]
    return jnp.concatenate(
        [
            lower_half * cosine_part - upper_half * sine_part,
            upper_half * cosine_part + lower_half * sine_part,
        ],
        axis=-1,
    )


def generic_body(
    ids,
    block_order,
    embed,
    mix_gain,
    in_proj,
    short_filter,
    long_filter,
    conv_skip,
    hyena_out,
    attn_gain,
    qkv_proj,
    attn_out,
):
    tok_rows = ids.shape[0]
    tensor_count = lax.axis_size("tensor")
    context_count = lax.axis_size("context")
    ctx_rows = tok_rows * tensor_count
    block_rows = ctx_rows // 2
    filter_len = long_filter.shape[1]
    short_len = short_filter.shape[1]
    halo_len = filter_len + short_len - 2
    chan_local = in_proj.shape[2]
    context_at = lax.axis_index("context")
    vocab_ids = jnp.arange(embed.shape[0], dtype=jnp.int32)
    chosen = (ids[:, None] == vocab_ids[None, :]).astype(jnp.bfloat16)
    embedded = jnp.dot(chosen, embed, preferred_element_type=jnp.float32).astype(jnp.bfloat16)
    embedded_all = lax.all_gather(embedded, "tensor", axis=0, tiled=True)
    mixed_in = rms_scale(embedded_all, mix_gain)
    projected = jnp.einsum(
        "rd,jdc->jrc", mixed_in, in_proj, preferred_element_type=jnp.float32
    ).astype(jnp.bfloat16)
    slot_ids = jnp.arange(2 * context_count, dtype=jnp.int32)
    slot_pair = 2 * context_at + jnp.arange(2, dtype=jnp.int32)
    owned_blocks = jnp.sum(
        jnp.where(slot_ids[None, :] == slot_pair[:, None], block_order[None, :], 0), axis=1
    )
    local_pos = (
        owned_blocks[:, None] * block_rows + jnp.arange(block_rows, dtype=jnp.int32)[None, :]
    ).reshape(ctx_rows)
    tail_rows = jnp.stack(
        [projected[:, block_rows - halo_len : block_rows], projected[:, ctx_rows - halo_len :]]
    )
    all_tails = lax.all_gather(tail_rows, "context", axis=0, tiled=True)
    out_len = filter_len - 1 + block_rows
    pieces = []
    for block_at in range(2):
        holder_hit = (block_order == owned_blocks[block_at] - 1).astype(jnp.bfloat16)
        before_rows = jnp.einsum(
            "s,sjrc->jrc", holder_hit, all_tails, preferred_element_type=jnp.float32
        )
        own_rows = projected[:, block_at * block_rows : (block_at + 1) * block_rows].astype(
            jnp.float32
        )
        extended = jnp.concatenate([before_rows, own_rows], axis=1)
        filtered = short_conv(extended, short_filter, out_len)
        gated_rows = filtered[1] * filtered[2]
        padded = jnp.concatenate([jnp.zeros((1, chan_local), jnp.float32), gated_rows], axis=0)
        long_mix = long_conv(padded, long_filter, GROUP_CH)
        own_gate = gated_rows[filter_len - 1 :]
        pieces.append(
            (filtered[0, filter_len - 1 :] * (long_mix + conv_skip * own_gate)).astype(jnp.bfloat16)
        )
    hyena_mix = jnp.concatenate(pieces, axis=0)
    hyena_own = lax.psum_scatter(
        jnp.dot(hyena_mix, hyena_out, preferred_element_type=jnp.float32),
        "tensor",
        scatter_dimension=0,
        tiled=True,
    )
    stream_own = embedded.astype(jnp.float32) + hyena_own
    stream_all = lax.all_gather(stream_own, "tensor", axis=0, tiled=True)
    attn_in = rms_scale(stream_all, attn_gain)
    projections = jnp.einsum("rd,jdf->jrf", attn_in, qkv_proj, preferred_element_type=jnp.float32)
    local_heads = projections.shape[2] // HD
    shaped = projections.reshape(3, ctx_rows, local_heads, HD)
    queries = rotate(shaped[0], local_pos, HD).astype(jnp.bfloat16)
    keys_flat = (
        rotate(shaped[1], local_pos, HD).astype(jnp.bfloat16).reshape(ctx_rows, local_heads * HD)
    )
    values_flat = shaped[2].astype(jnp.bfloat16).reshape(ctx_rows, local_heads * HD)
    score_scale = HD ** (-0.5)
    start_state = (
        jnp.full((2, block_rows, local_heads), NEG_FILL, jnp.float32),
        jnp.zeros((2, block_rows, local_heads), jnp.float32),
        jnp.zeros((2, block_rows, local_heads, HD), jnp.float32),
    )
    key_piece = lax.all_gather(keys_flat, "context", axis=0, tiled=True)
    value_piece = lax.all_gather(values_flat, "context", axis=0, tiled=True)
    piece_len = key_piece.shape[0]
    sub_len = math.gcd(piece_len, 512)

    def attend_sub(sub_index, carried):
        key_block = lax.dynamic_slice_in_dim(key_piece, sub_index * sub_len, sub_len, 0).reshape(
            sub_len, local_heads, HD
        )
        value_block = lax.dynamic_slice_in_dim(
            value_piece, sub_index * sub_len, sub_len, 0
        ).reshape(sub_len, local_heads, HD)
        row_ids = sub_index * sub_len + jnp.arange(sub_len, dtype=jnp.int32)
        holder = row_ids // block_rows
        key_pos = (
            jnp.sum(
                jnp.where(holder[:, None] == slot_ids[None, :], block_order[None, :], 0), axis=1
            )
            * block_rows
            + row_ids % block_rows
        )
        top_all, sums_all, weighted_all = carried
        outputs = []
        for block_at in range(2):
            query_rows = queries[block_at * block_rows : (block_at + 1) * block_rows]
            query_pos = local_pos[block_at * block_rows : (block_at + 1) * block_rows]
            top_score = top_all[block_at]
            weight_sum = sums_all[block_at]
            weighted = weighted_all[block_at]
            scores = (
                jnp.einsum(
                    "qhd,khd->qhk", query_rows, key_block, preferred_element_type=jnp.float32
                )
                * score_scale
            )
            visible = key_pos[None, None, :] <= query_pos[:, None, None]
            scores = jnp.where(visible, scores, NEG_FILL)
            new_top = jnp.maximum(top_score, jnp.max(scores, axis=-1))
            rescale = jnp.exp(top_score - new_top)
            weights = jnp.where(visible, jnp.exp(scores - new_top[..., None]), 0.0)
            weight_sum = weight_sum * rescale + jnp.sum(weights, axis=-1)
            weighted = weighted * rescale[..., None] + jnp.einsum(
                "qhk,khd->qhd",
                weights.astype(jnp.bfloat16),
                value_block,
                preferred_element_type=jnp.float32,
            )
            result = (new_top, weight_sum, weighted)
            outputs.append(result)
        return tuple((jnp.stack([entry[field] for entry in outputs]) for field in range(3)))

    _, sums_final, weighted_final = lax.fori_loop(0, piece_len // sub_len, attend_sub, start_state)
    attended = (
        (weighted_final / sums_final[..., None])
        .astype(jnp.bfloat16)
        .reshape(ctx_rows, local_heads * HD)
    )
    attn_own = lax.psum_scatter(
        jnp.dot(attended, attn_out, preferred_element_type=jnp.float32).astype(jnp.bfloat16),
        "tensor",
        scatter_dimension=0,
        tiled=True,
    ).astype(jnp.float32)
    return stream_own + attn_own


CODES = (65, 67, 71, 84)
BF16 = jnp.bfloat16
F32 = jnp.float32
VM = pl.BlockSpec(memory_space=pltpu.VMEM)
SM = pl.BlockSpec(memory_space=pltpu.SMEM)

UNIT, CTX, PLANE, CROSS, HALF = 0, 4, 8, 12, 13
MINE, THEIRS, SLOTS = 15, 17, 19


def position_table():
    rows = []
    for half in range(2):
        for ctx in range(4):
            for plane in range(4):
                units = [plane, (1, 0, 3, 2)[plane], (2, 2, 1, 1)[plane], (3, 3, 0, 0)[plane]]
                row = units + [ctx ^ rel for rel in range(4)] + [plane ^ rel for rel in range(4)]
                row += [(ctx & 1) ^ (ctx >> 1), half, 1 - half]
                row += [2 * half, 2 * half + 1, 2 - 2 * half, 3 - 2 * half]
                row += [2 * (ctx ^ rel) + at for rel in range(4) for at in range(2)]
                rows.append(row)
    return np.array(rows, np.int32)


def swap(value, axis, mask):
    size = lax.axis_size(axis)
    return lax.ppermute(value, axis, [(at, at ^ mask) for at in range(size)])


def rows_of(weights, lane_start, width):
    return lax.dynamic_slice(weights, (0, lane_start), (weights.shape[0], width))


def along_chain(piece, edge_plane):
    middle = [(1, 2), (2, 1)]
    outward = [(1, 0), (2, 3)]
    near = swap(piece, "tensor", 1)
    across = lax.ppermute(piece, "tensor", middle)
    far_mid = lax.ppermute(near, "tensor", middle)
    across_out = lax.ppermute(across, "tensor", outward)
    far_out = lax.ppermute(far_mid, "tensor", outward)
    return (
        near,
        jnp.where(edge_plane, across_out, across),
        jnp.where(edge_plane, far_out, far_mid),
    )


def dot32(left, right):
    return jnp.dot(left, right, preferred_element_type=F32)


def down_rows(left, right):
    return lax.dot_general(
        left, right, (((0,), (0,)), ((), ())), preferred_element_type=F32
    )


def hyena_kernel(where_ref, coef_ref, hot_ref, taps_ref, mix_ref):
    hot = hot_ref[...]
    first, second, third = (down_rows(coef_ref[j], hot) for j in range(3))
    skip = down_rows(coef_ref[3], jnp.ones((coef_ref.shape[1], 512), BF16))
    gated = second * third
    packed = gated.astype(BF16)
    row = lax.broadcasted_iota(jnp.int32, (128, 128), 0)
    lane = lax.broadcasted_iota(jnp.int32, (128, 128), 1)
    near = lane >= row
    mixed = []
    for group in range(16):
        spread = jnp.broadcast_to(taps_ref[group : group + 1, :], (128, 128))
        rolled = pltpu.roll(spread, 0, 1, stride=1, stride_axis=0)
        zero = jnp.zeros_like(rolled)
        matrix = jnp.concatenate(
            [jnp.where(near, zero, rolled), jnp.where(near, rolled, zero)], axis=0
        ).astype(BF16)
        chans = packed[16 * group : 16 * group + 16]
        left = jnp.concatenate(
            [chans[:, at : at + 256] for at in (0, 128, 384, 512)], axis=0
        )
        result = dot32(left, matrix)
        mixed.append(jnp.concatenate([result[16 * i : 16 * i + 16] for i in range(4)], axis=1))
    long_mix = jnp.concatenate(mixed, axis=0)
    own_gate = jnp.concatenate([gated[:, 128:384], gated[:, 512:768]], axis=1)
    own_first = jnp.concatenate([first[:, 128:384], first[:, 512:768]], axis=1)
    mix = own_first * (long_mix + skip * own_gate)
    mix_ref[...] = mix.T.astype(BF16)


def hyena_mixes(where, coef, hot, taps):
    chans = coef.shape[2]
    step = 256
    return pl.pallas_call(
        hyena_kernel,
        grid_spec=pltpu.PrefetchScalarGridSpec(
            num_scalar_prefetch=1,
            grid=(chans // step,),
            in_specs=[
                pl.BlockSpec((4, coef.shape[1], step), lambda i, w: (0, 0, i)),
                pl.BlockSpec(hot.shape, lambda i, w: (0, 0)),
                pl.BlockSpec((step // 16, 128), lambda i, w: (i, 0)),
            ],
            out_specs=pl.BlockSpec(
                (512, step), lambda i, w: (0, w[PLANE + i // 2] * 2 + i % 2)
            ),
        ),
        out_shape=jax.ShapeDtypeStruct((512, chans), BF16),
        name="hyena_mix",
    )(where, coef, hot, taps)


def both(own_ref, oth_ref):
    return jnp.concatenate([own_ref[...], oth_ref[...]], axis=0)


def branch_lane(where_ref, rel):
    return pl.ds(pl.multiple_of(where_ref[CTX + rel] * 512, 512), 512)


def branch_a_kernel(where_ref, own0, oth0, own1, oth1, own2, oth2, home_ref, *refs):
    block1, block2, sum_ref = refs[:5], refs[5:9], refs[9]
    left0, left1, left2 = both(own0, oth0), both(own1, oth1), both(own2, oth2)
    rows = own0.shape[0]
    for rel in range(4):
        lane = branch_lane(where_ref, rel)
        total = dot32(left0, home_ref[:, lane])
        if rel < 3:
            total += dot32(left1, block1[rel][...])
        else:
            total += dot32(left1[:, :256], block1[3][...])
            total += dot32(left1[:, 256:], block1[4][...])
        total += dot32(left2, block2[rel][...])
        sum_ref[0, :, lane] = total[:rows]
        sum_ref[1, :, lane] = total[rows:]


def branch_b_kernel(where_ref, own3, oth3, sum_ref, *refs):
    block3, (own_ref, oth_ref) = refs[:4], refs[4:]
    left3 = both(own3, oth3)
    rows = own3.shape[0]
    for rel in range(4):
        lane = branch_lane(where_ref, rel)
        total = dot32(left3, block3[rel][...])
        own_ref[:, lane] = sum_ref[0, :, lane] + total[:rows]
        oth_ref[:, lane] = (sum_ref[1, :, lane] + total[rows:]).astype(BF16)


def hyena_branches(where, own_mix, oth_mix, home, parts):
    tile = 256
    grid = (512 // tile,)

    def mixes(at):
        return [pl.BlockSpec((tile, 512), lambda i, w: (i, w[UNIT + at]))] * 2

    sums = pl.BlockSpec((2, tile, 2048), lambda i, w: (0, i, 0))
    flat = pl.BlockSpec((tile, 2048), lambda i, w: (i, 0))
    sum_shape = jax.ShapeDtypeStruct((2, 512, 2048), F32)
    half_shapes = [
        jax.ShapeDtypeStruct((512, 2048), F32),
        jax.ShapeDtypeStruct((512, 2048), BF16),
    ]

    def call(kernel, in_specs, out_specs, out_shape, operands):
        return pl.pallas_call(
            kernel,
            grid_spec=pltpu.PrefetchScalarGridSpec(
                num_scalar_prefetch=1, grid=grid, in_specs=in_specs, out_specs=out_specs
            ),
            out_shape=out_shape,
            name="hyena_branch",
        )(where, *operands)

    mix = [own_mix, oth_mix]
    home_spec = pl.BlockSpec((512, 2048), lambda i, w: (0, w[HALF]))
    partial = call(
        branch_a_kernel,
        mixes(0) + mixes(1) + mixes(2) + [home_spec] + [VM] * 9,
        sums,
        sum_shape,
        mix * 3 + [home] + parts[0] + parts[1],
    )
    return call(
        branch_b_kernel,
        mixes(3) + [sums] + [VM] * 4,
        [flat, flat],
        half_shapes,
        mix + [partial] + parts[2],
    )


def qkv_kernel(where_ref, half_ref, hot_ref, base_ref, gain_ref, proj_ref, *refs, first):
    at = pl.program_id(0)
    if first:
        total_ref, power_ref, rows_ref, block_ref = refs
    else:
        part_ref, part_power_ref, cos_ref, sin_ref = refs[:4]
        head_refs = refs[4:8]
        rows_ref, total_ref, power_ref, block_ref = refs[8:]

    @pl.when(at == 0)
    def _():
        if first:
            total_ref[...] = jnp.zeros_like(total_ref)
            power_ref[...] = jnp.zeros_like(power_ref)
        else:
            total_ref[...] = part_ref[...]
            power_ref[...] = part_power_ref[...]

    stream = dot32(hot_ref[...], base_ref[...]) + half_ref[...].astype(F32)
    block_ref[...] = stream
    rows_ref[...] = block_ref[pl.ds(pl.multiple_of(where_ref[PLANE] * 128, 128), 128), :]
    power_ref[...] += jnp.sum(stream * stream, axis=1, keepdims=True)
    scaled = (stream * gain_ref[...]).astype(BF16)
    for j in range(3):
        total_ref[:, 512 * j : 512 * j + 512] += dot32(scaled, proj_ref[j])
    if first:
        return

    @pl.when(at == 1)
    def _():
        factor = lax.rsqrt(power_ref[...] * (1.0 / 4096.0) + EPS)
        cosine = cos_ref[...] * factor
        sine = sin_ref[...] * factor
        for rel in range(4):
            for j in range(3):
                lane = pl.multiple_of(where_ref[CTX + rel] * 128 + 512 * j, 128)
                piece = total_ref[:, pl.ds(lane, 128)]
                if j < 2:
                    piece = piece * cosine + pltpu.roll(piece, 64, 1) * sine
                else:
                    piece = piece * factor
                head_refs[rel][:, 128 * j : 128 * j + 128] = piece.astype(BF16)


def qkv_half(where, half, hot, base, gain, proj, extra=()):
    first = not extra
    at = MINE if first else THEIRS
    whole = lambda shape: pl.BlockSpec(shape, lambda i, w: (0,) * len(shape))
    in_specs = [
        pl.BlockSpec((512, 1024), lambda i, w: (0, i)),
        whole(hot.shape),
        pl.BlockSpec((base.shape[0], 1024), lambda i, w: (0, w[at + i])),
        pl.BlockSpec((1, 1024), lambda i, w: (0, w[at + i])),
        pl.BlockSpec((3, 1024, 512), lambda i, w: (0, w[at + i], 0)),
    ]
    rows_spec = pl.BlockSpec((128, 1024), lambda i, w: (0, i))
    rows_shape = jax.ShapeDtypeStruct((128, 2048), F32)
    scratch = [pltpu.VMEM((512, 1024), F32)]
    if first:
        out_specs = [whole((512, 1536)), whole((512, 1)), rows_spec]
        out_shape = [
            jax.ShapeDtypeStruct((512, 1536), F32),
            jax.ShapeDtypeStruct((512, 1), F32),
            rows_shape,
        ]
    else:
        in_specs += [whole(value.shape) for value in extra]
        out_specs = [whole((512, 384))] * 4 + [rows_spec]
        out_shape = [jax.ShapeDtypeStruct((512, 384), BF16)] * 4 + [rows_shape]
        scratch = [pltpu.VMEM((512, 1536), F32), pltpu.VMEM((512, 1), F32)] + scratch
    return pl.pallas_call(
        functools.partial(qkv_kernel, first=first),
        grid_spec=pltpu.PrefetchScalarGridSpec(
            num_scalar_prefetch=1,
            grid=(2,),
            in_specs=in_specs,
            out_specs=out_specs,
            scratch_shapes=scratch,
        ),
        out_shape=out_shape,
        name="qkv_half",
    )(where, half, hot, base, gain, proj, *extra)


def attend_kernel(slot_ref, *refs):
    x_refs, out_refs, (q_ref, k_ref, v_ref, mixed_ref) = refs[:4], refs[4:8], refs[8:]
    for rel, x_ref in enumerate(x_refs):
        for half in range(2):
            base = pl.multiple_of(slot_ref[2 * rel + half] * 256, 256)
            rows = slice(256 * half, 256 * half + 256)
            q_ref[pl.ds(base, 256), :] = x_ref[rows, 0:128]
            k_ref[pl.ds(base, 256), :] = x_ref[rows, 128:256]
            v_ref[pl.ds(base, 256), :] = x_ref[rows, 256:384]
    row = lax.broadcasted_iota(jnp.int32, (256, 256), 0)
    lane = lax.broadcasted_iota(jnp.int32, (256, 256), 1)
    causal = lane <= row
    scale = HD ** (-0.5)
    for block in range(8):
        width = 256 * block + 256
        query = q_ref[256 * block : width, :]
        scores = lax.dot_general(
            query, k_ref[0:width, :], (((1,), (1,)), ((), ())), preferred_element_type=F32
        )
        last = jnp.where(causal, scores[:, width - 256 :], NEG_FILL)
        if block > 0:
            scores = jnp.concatenate([scores[:, : width - 256], last], axis=1)
        else:
            scores = last
        top = jnp.max(scores, axis=1, keepdims=True)
        weights = jnp.exp((scores - top) * scale)
        total = jnp.sum(weights, axis=1, keepdims=True)
        mixed = dot32(weights.astype(BF16), v_ref[0:width, :])
        mixed_ref[256 * block : width, :] = (mixed / total).astype(BF16)
    for rel, out_ref in enumerate(out_refs):
        for half in range(2):
            base = pl.multiple_of(slot_ref[2 * rel + half] * 256, 256)
            out_ref[256 * half : 256 * half + 256, :] = mixed_ref[pl.ds(base, 256), :]


def attend(slots, pieces):
    return pl.pallas_call(
        attend_kernel,
        in_specs=[SM] + [VM] * 4,
        out_specs=[VM] * 4,
        out_shape=[jax.ShapeDtypeStruct((512, 128), BF16)] * 4,
        scratch_shapes=[pltpu.VMEM((2048, 128), BF16)] * 4,
        name="attend",
    )(slots, *pieces)


def out_kernel(where_ref, own_ref, oth_ref, rows_ref, home_ref, *refs):
    parts, refs = refs[:9], refs[9:]
    own_out_ref, oth_out_ref, left_ref, home_vm, *rest = refs
    held, sem = rest[:9], rest[9]
    lane = pl.multiple_of(where_ref[HALF] * 2048, 2048)
    copies = [pltpu.make_async_copy(home_ref.at[:, pl.ds(lane, 2048)], home_vm, sem.at[9])]
    copies += [
        pltpu.make_async_copy(part, room, sem.at[at])
        for at, (part, room) in enumerate(zip(parts, held))
    ]
    copies[0].start()
    for kind in range(3):
        for unit in range(3):
            copies[1 + 3 * unit + kind].start()
    for side, src_ref in enumerate((own_ref, oth_ref)):
        for far in range(4):
            for rel in range(4):
                head = where_ref[PLANE + far] * 4 + where_ref[CTX + rel]
                lane = pl.multiple_of(head * 128, 128)
                at = 512 * far + 128 * rel
                left_ref[128 * side : 128 * side + 128, pl.ds(lane, 128)] = src_ref[
                    :, at : at + 128
                ]

    def left(unit):
        return left_ref[:, pl.ds(pl.multiple_of(where_ref[UNIT + unit] * 512, 512), 512)]

    lanes = []
    copies[0].wait()
    for quarter in range(4):
        half = where_ref[CROSS] if quarter < 2 else 1 - where_ref[CROSS]
        lanes.append(pl.multiple_of(half * 1024 + (quarter % 2) * 512, 512))
        own_out_ref[:, pl.ds(lanes[quarter], 512)] = rows_ref[:, pl.ds(lanes[quarter], 512)]
    for quarter in range(4):
        for unit in range(3):
            if quarter != 1:
                copies[1 + 3 * unit + max(quarter - 1, 0)].wait()
        total = dot32(left(0), home_vm[:, pl.ds(lanes[quarter], 512)])
        for unit in range(3):
            block, side_x, side_y = held[3 * unit : 3 * unit + 3]
            if quarter < 2:
                right = block[:, 512 * quarter : 512 * quarter + 512]
            else:
                right = (side_x, side_y)[quarter - 2][...]
            total += dot32(left(unit + 1), right)
        own_out_ref[:, pl.ds(lanes[quarter], 512)] += total[:128]
        oth_out_ref[:, pl.ds(lanes[quarter], 512)] = total[128:].astype(oth_out_ref.dtype)


def out_branches(where, own, oth, rows, home, parts):
    anywhere = pl.BlockSpec(memory_space=pl.ANY)
    flat = pl.BlockSpec((128, 2048), lambda i, w: (0, 0))
    return pl.pallas_call(
        out_kernel,
        grid_spec=pltpu.PrefetchScalarGridSpec(
            num_scalar_prefetch=1,
            grid=(1,),
            in_specs=[flat, flat, flat] + [anywhere] * (1 + len(parts)),
            out_specs=[pl.BlockSpec((128, 2048), lambda i, w: (0, w[HALF])), flat],
            scratch_shapes=[pltpu.VMEM((256, 2048), BF16), pltpu.VMEM((512, 2048), BF16)]
            + [pltpu.VMEM(part.shape, BF16) for part in parts]
            + [pltpu.SemaphoreType.DMA((10,))],
        ),
        out_shape=[jax.ShapeDtypeStruct((128, 4096), F32), jax.ShapeDtypeStruct((128, 2048), BF16)],
        name="out_branch",
    )(where, own, oth, rows, home, *parts)


def block_body(*operands):
    return block_rows_out(*operands)


def block_rows_out(
    ids,
    block_order,
    embed,
    mix_gain,
    in_proj,
    short_filter,
    long_filter,
    conv_skip,
    hyena_out,
    attn_gain,
    qkv_proj,
    attn_out,
):
    half_at = lax.axis_index("dp")
    ctx = lax.axis_index("context")
    plane = lax.axis_index("tensor")
    edge = jnp.logical_or(plane == 0, plane == 3)
    order = block_order.astype(jnp.int32)
    half_lane = half_at * 2048
    table_rows = jnp.asarray(position_table())
    where = lax.dynamic_index_in_dim(table_rows, half_at * 16 + ctx * 4 + plane, 0, keepdims=False)

    piece = rows_of(hyena_out, half_lane + ctx * 512, 512)
    parts = []
    for at, unit in enumerate(along_chain(piece, edge)):
        side_x = swap(unit, "context", 1)
        side_y = swap(unit, "context", 2)
        if at == 0:
            corner = [swap(side_y[:256], "context", 1), swap(side_x[256:], "context", 2)]
        else:
            corner = [swap(unit, "context", 3)]
        parts.append([unit, side_x, side_y] + corner)

    own_row = ids.astype(F32).reshape(1, 128)
    id_rows = jnp.concatenate(
        [own_row] + [swap(own_row, "context", rel) for rel in range(1, 4)], axis=1
    )

    base = jnp.concatenate([embed[code : code + 1] for code in CODES], axis=0)
    mixed_in = rms_scale(base, mix_gain)
    table = jnp.einsum(
        "rd,jdc->jrc", mixed_in, in_proj, preferred_element_type=F32
    ).astype(BF16)
    packed = jnp.concatenate(
        [
            table.astype(F32).reshape(12, 512),
            short_filter.reshape(9, 512),
            conv_skip.reshape(1, 512),
            long_filter.reshape(8, 512),
            id_rows,
        ],
        axis=0,
    )
    everything = jnp.stack([packed] + [swap(packed, "tensor", rel) for rel in range(1, 4)])
    slot_ids = jnp.arange(8, dtype=jnp.int32)
    place = jnp.sum(
        jnp.where(where[SLOTS : SLOTS + 8, None] == slot_ids[None, :], order[None, :], 0), axis=1
    )
    owned = place[:2]
    local_pos = (
        owned[:, None] * 256 + jnp.arange(256, dtype=jnp.int32)[None, :]
    ).reshape(512)
    inverse_freq = THETA ** (-(2.0 * jnp.arange(64, dtype=F32)) / HD)
    angles = local_pos.astype(F32)[:, None] * inverse_freq[None, :]
    cosine = jnp.cos(angles)
    sine = jnp.sin(angles)
    cosine = jnp.concatenate([cosine, cosine], axis=1)
    sine = jnp.concatenate([-sine, sine], axis=1)
    which = where[None, PLANE : PLANE + 4] == jnp.arange(4, dtype=jnp.int32)[:, None]
    plane_ids = everything[:, 30].reshape(1, 4, 4, 128)
    plane_ids = jnp.sum(jnp.where(which[:, :, None, None], plane_ids, 0.0), axis=1)
    all_ids = plane_ids.transpose(1, 0, 2).reshape(8, 256)
    tables = everything[:, :12].reshape(4, 3, 1, 4, 512)
    shorts = everything[:, 12:21].reshape(4, 3, 3, 1, 512)
    coef = (tables * shorts).transpose(1, 2, 3, 0, 4).reshape(3, 12, 2048)
    skip = everything[:, 21].reshape(1, 1, 2048)
    coef = jnp.concatenate(
        [
            jnp.pad(coef, ((0, 0), (0, 4), (0, 0))),
            jnp.pad(skip, ((0, 0), (0, 15), (0, 0))),
        ],
        axis=0,
    )
    coarse = lax.reduce_precision(coef, 8, 7)
    coef = jnp.concatenate([coarse, coef - coarse], axis=1).astype(BF16)
    taps = everything[:, 22:30].reshape(128, 128)

    before_hit = place[None, :] == owned[:, None] - 1
    own_ids = all_ids[:2]
    before_ids = jnp.sum(jnp.where(before_hit[:, :, None], all_ids[None], 0.0), axis=1)
    span = jnp.concatenate([before_ids, own_ids], axis=1)
    codes = jnp.array(CODES, F32)
    hot = jnp.stack(
        [
            (span[None, :, 128 - lag : 512 - lag] == codes[:, None, None]).astype(BF16)
            for lag in range(3)
        ]
    ).reshape(12, 768)
    hot = jnp.pad(hot, ((0, 4), (0, 0)))
    hot = jnp.concatenate([hot, hot], axis=0)
    own_hot = (own_ids.reshape(512, 1) == codes[None, :]).astype(BF16)
    coef, hot, place, cosine, sine, own_hot, base = lax.optimization_barrier(
        (coef, hot, place, cosine, sine, own_hot, base)
    )

    own_mix = hyena_mixes(where, coef, hot, taps)
    oth_mix = swap(own_mix, "dp", 1)

    own_half, give_half = hyena_branches(where, own_mix, oth_mix, hyena_out, parts)
    got_half = swap(give_half, "dp", 1)
    gain = attn_gain[None]
    total, power, own_rows = qkv_half(where, own_half, own_hot, base, gain, qkv_proj)
    *heads, oth_rows = qkv_half(
        where, got_half, own_hot, base, gain, qkv_proj, (total, power, cosine, sine)
    )

    pieces = [heads[0]] + [swap(heads[rel], "context", rel) for rel in range(1, 4)]
    attended = attend(place, pieces)
    mine = jnp.concatenate(
        [attended[0]]
        + [swap(attended[rel], "context", rel) for rel in range(1, 4)],
        axis=1,
    ).reshape(4, 128, 512)

    def rows_for(rel):
        return lax.dynamic_index_in_dim(mine, plane ^ rel, 0, keepdims=False)

    own_att = jnp.concatenate(
        [rows_for(0)] + [swap(rows_for(rel), "tensor", rel) for rel in range(1, 4)],
        axis=1,
    )
    oth_att = swap(own_att, "dp", 1)

    cross = (ctx & 1) ^ (ctx >> 1)
    late_lane, _ = lax.optimization_barrier((half_lane + cross * 1024, coef))
    units = along_chain(rows_of(attn_out, late_lane, 1024), edge)
    parts = []
    for unit in units:
        parts += [unit, swap(unit[:, :512], "context", 1), swap(unit[:, 512:], "context", 2)]
    own_out, give_out = out_branches(where, own_att, oth_att, own_rows, attn_out, parts)
    got_out = swap(give_out, "dp", 1)
    return lax.dynamic_update_slice(
        own_out, oth_rows + got_out.astype(F32), (0, (1 - half_at) * 2048)
    )


def solution(mesh):
    grid_shape = dict(mesh.shape)
    square = (grid_shape["dp"], grid_shape["context"], grid_shape["tensor"]) == (2, 4, 4)
    body = block_body if square else generic_body
    placed = (
        P(("dp", "context", "tensor")),
        P("dp"),
        P(),
        P(),
        P(None, None, "tensor"),
        P(None, None, "tensor"),
        P("tensor", None),
        P("tensor"),
        P("tensor", None),
        P(),
        P(None, None, "tensor"),
        P("tensor", None),
    )
    return jax.shard_map(
        body,
        mesh=mesh,
        in_specs=placed,
        out_specs=P(("dp", "context", "tensor"), None),
        check_vma=False,
    )
```
